128 devices in a mesh: row: 8 (over y, core), col: 16 (over x, z).
Axes of the slice: x: 4, y: 4, z: 4, core: 2. Of those that a mesh axis runs over, the one named last changes fastest.
Arguments:
- object_field: float32 [2, 2048, 4096], P(None, 'row', 'col'), may hold values from -4.2 to 4.2
- probe_modes: float32 [2, 8, 256, 256], replicated, may hold values from -1.5 to 1.5
- patterns: float32 [256, 256, 256], P(('row', 'col')), may hold values from 0.3 to 3
- offsets: int32 [2, 256], P(None, ('row', 'col')), may hold values from 0 to 3840, as said below
- counts: int32 [128], P(('row', 'col')), may hold values from 1 to 2, as said below
Outputs:
- new_object: float32 [2, 2048, 4096], P(None, 'row', 'col')
- new_probe: float32 [2, 8, 256, 256], replicated
The draws below stay inside these ranges and needn't reach their ends.
Inputs may be any that keep to these rules, and one draw needn't show every extreme that they name: `offsets`: A slot of the device of tile row r and tile column c has row offset in [r * 256, (r + 1) * 256) and column offset in [c * 256, (c + 1) * 256); every patch lies inside the object. `counts`: A device's live slots are its first ones.
All inputs are finite; a program needn't handle non-finite values.
Results may differ from the reference program's by a relative error of at most 0.0001.
Values sent between devices are 32-bit elements; how exact they have to be, the bound alone decides.
No kernel may reach another device: no remote copies, remote signals or barrier semaphores. Data moves between devices by JAX's collectives and lax.ppermute only.
A program may use at most 128 MiB of HBM per device.

```python
import math
import jax
import jax.numpy as jnp
from jax import lax

FRAME = 256
MODES = 8
TILE = 256
SLOTS = 2
HEIGHT = 2048
WIDTH = 4096
POSITIONS = 256
N_ROW = 8
N_COL = 16


def draw_offsets(key, part):
    total = N_ROW * N_COL * SLOTS
    slot_ids = jnp.arange(total, dtype=jnp.int32)
    device_ids = slot_ids // SLOTS
    tile_row = device_ids // N_COL
    tile_col = device_ids % N_COL
    height_all = TILE * N_ROW
    width_all = TILE * N_COL
    limit_row = jnp.minimum(TILE, height_all - FRAME - tile_row * TILE + 1)
    limit_col = jnp.minimum(TILE, width_all - FRAME - tile_col * TILE + 1)
    first_key = jax.random.fold_in(key, 11)
    second_key = jax.random.fold_in(key, 23)
    raw_row = jax.random.randint(first_key, (total,), 0, 1 << 30, dtype=jnp.int32)
    raw_col = jax.random.randint(second_key, (total,), 0, 1 << 30, dtype=jnp.int32)
    row_offset = tile_row * TILE + raw_row % limit_row
    col_offset = tile_col * TILE + raw_col % limit_col
    row_offset = jnp.where(slot_ids == 0, 0, row_offset)
    col_offset = jnp.where(slot_ids == 0, 0, col_offset)
    row_offset = jnp.where(slot_ids == total - 1, height_all - FRAME, row_offset)
    col_offset = jnp.where(slot_ids == total - 1, width_all - FRAME, col_offset)
    return jnp.stack([row_offset, col_offset]).astype(jnp.int32)


def draw_counts(key, part):
    devices_all = N_ROW * N_COL
    fewest = max(1, SLOTS - 1)
    drawn = jax.random.randint(jax.random.fold_in(key, 37), (devices_all,), fewest, SLOTS + 1, dtype=jnp.int32)
    drawn = drawn.at[0].set(SLOTS)
    drawn = drawn.at[devices_all - 1].set(fewest)
    return drawn.astype(jnp.int32)


def levels(own_key, shape, split, least, high):
    def one(dim, shards_of):
        draws = jax.random.uniform(jax.random.fold_in(jax.random.fold_in(own_key, 6), dim), (shards_of,), jnp.float32, least / len(split), high / len(split))
        return jnp.repeat(jnp.exp(draws), shape[dim] // shards_of).reshape((-1,) + (1,) * (len(shape) - dim - 1))

    level = one(*split[0])
    for cut in split[1:]:
        level = level * one(*cut)
    return level


def bell_draw(own_key, extent, scale, limit, shards=(), kind=jnp.bfloat16):
    result = jax.random.normal(own_key, extent, jnp.float32) * scale
    if len(shards) > 0:
        result = levels(own_key, extent, shards, -0.22, 0.18) * result
    return jnp.clip(result, min=-limit, max=limit).astype(kind)


def setup_inputs(seed: int = 0) -> dict:
    seeds = jax.random.split(jax.random.key(seed), 6)
    return {
        "object_field": bell_draw(seeds[0], (2, HEIGHT, WIDTH), 0.7, 4.2, ((1, 8), (2, 16)), jnp.float32),
        "probe_modes": bell_draw(seeds[1], (2, MODES, FRAME, FRAME), 0.25, 1.5, (), jnp.float32),
        "patterns": jnp.clip(jnp.exp(math.log(3.0) - 2.3025851 * jax.random.uniform(seeds[2], (POSITIONS, FRAME, FRAME), jnp.float32) ** levels(seeds[2], (POSITIONS, FRAME, FRAME), ((0, 128),), -0.2, 0.2)), 0.3, 3.0),
        "offsets": draw_offsets(jax.random.fold_in(seeds[5], 71), 0),
        "counts": draw_counts(jax.random.fold_in(seeds[5], 71), 0),
    }


INTENSITY_FLOOR = 0.1
OBJECT_DELTA = 0.5
PROBE_DELTA = 1.0
SMOOTH_WEIGHT = 0.1

def reference(object_field, probe_modes, patterns, offsets, counts):
    float_type = object_field.dtype
    object_now = lax.complex(object_field[0], object_field[1])
    probe_field = lax.complex(probe_modes[0], probe_modes[1])
    probe_power = lax.optimization_barrier(jnp.sum(probe_modes[0] * probe_modes[0] + probe_modes[1] * probe_modes[1], axis=0))

    def visit_position(position, running):
        numerator, illumination, gradient, object_power = running
        position = jnp.asarray(position).astype(jnp.int32)
        row_start = offsets[0, position].astype(jnp.int32)
        col_start = offsets[1, position].astype(jnp.int32)
        live_flag = (position % SLOTS < counts[position // SLOTS]).astype(float_type)
        object_patch = lax.dynamic_slice(object_now, (row_start, col_start), (FRAME, FRAME))
        exit_wave = probe_field * object_patch[None]
        spectrum = jnp.fft.fft2(exit_wave, norm='ortho')
        intensity = lax.optimization_barrier(jnp.sum(jnp.real(spectrum) * jnp.real(spectrum) + jnp.imag(spectrum) * jnp.imag(spectrum), axis=0))
        scale_ratio = patterns[position] / jnp.sqrt(jnp.maximum(intensity, INTENSITY_FLOOR))
        revised = jnp.fft.ifft2(spectrum * scale_ratio[None], norm='ortho')
        difference = (revised - exit_wave) * live_flag
        numer_piece = lax.optimization_barrier(jnp.sum(jnp.conj(probe_field) * difference, axis=0))
        current = lax.dynamic_slice(numerator, (row_start, col_start), (FRAME, FRAME))
        numerator = lax.dynamic_update_slice(numerator, current + numer_piece, (row_start, col_start))
        current_light = lax.dynamic_slice(illumination, (row_start, col_start), (FRAME, FRAME))
        illumination = lax.dynamic_update_slice(illumination, current_light + live_flag * probe_power, (row_start, col_start))
        gradient = gradient + jnp.conj(object_patch)[None] * difference
        patch_power = jnp.real(object_patch) * jnp.real(object_patch) + jnp.imag(object_patch) * jnp.imag(object_patch)
        object_power = object_power + live_flag * patch_power
        return (numerator, illumination, gradient, object_power)
    initial = (jnp.zeros_like(object_now), jnp.zeros((HEIGHT, WIDTH), float_type), jnp.zeros_like(probe_field), jnp.zeros((FRAME, FRAME), float_type))
    numerator, illumination, gradient, object_power = lax.fori_loop(0, POSITIONS, visit_position, initial)
    updated = object_now + numerator / (illumination + OBJECT_DELTA)
    padded = jnp.pad(updated, 1)
    neighbours = padded[2:, 1:-1] + padded[:-2, 1:-1] + padded[1:-1, 2:] + padded[1:-1, :-2]
    smoothed = updated + SMOOTH_WEIGHT * (neighbours - 4.0 * updated)
    probe_next = probe_field + gradient / (object_power + PROBE_DELTA)
    return (jnp.stack([jnp.real(smoothed), jnp.imag(smoothed)]), jnp.stack([jnp.real(probe_next), jnp.imag(probe_next)]))
```

```python
import math

import jax
import jax.numpy as jnp
import numpy as np
from jax import lax
from jax.experimental import pallas as pl
from jax.experimental.pallas import tpu as pltpu
from jax.sharding import PartitionSpec as P

INTENSITY_FLOOR = 0.1
OBJECT_DELTA = 0.5
PROBE_DELTA = 1.0
SMOOTH_WEIGHT = 0.1
FRAME = 256
HALF = 128
MODES = 8
F32 = jnp.float32
BF16 = jnp.bfloat16
PARAMS = pltpu.CompilerParams(vmem_limit_bytes=60000 * 1024)


def tables():
    k = np.arange(HALF)[:, None] + 0.5
    x = np.arange(FRAME)[None, :]
    angle = 2.0 * math.pi * k * x / FRAME
    packed = np.concatenate([np.cos(angle), np.sin(angle)], axis=0) / math.sqrt(FRAME)
    high = packed.astype(np.float32).astype(jnp.bfloat16)
    low = (packed - high.astype(np.float64)).astype(np.float32).astype(jnp.bfloat16)
    ramp = np.arange(FRAME)
    phase = math.pi * (ramp[:, None] + ramp[None, :]) / FRAME
    mod = np.stack([np.cos(phase), np.sin(phase)]).astype(np.float32)
    return (high, low, high.T.copy(), low.T.copy()), mod


def full(*shape):
    return pl.BlockSpec(shape, lambda m: (0,) * len(shape))


def smem():
    return pl.BlockSpec(memory_space=pltpu.SMEM)


def vmem():
    return pl.BlockSpec(memory_space=pltpu.VMEM)


def shape_of(*shape):
    return jax.ShapeDtypeStruct(shape, F32)


def split(value):
    high = value.astype(BF16)
    return high, (value - high.astype(F32)).astype(BF16)


def mm(a, b):
    return jnp.dot(a, b, preferred_element_type=F32)


def two_sided(real, imag, left, right):
    rows = real.shape[0]
    high, low = split(jnp.concatenate([real, imag], axis=0))
    first = mm(high, right[0]) + mm(low, right[0]) + mm(high, right[1])
    results = []
    for part in (first[:rows], first[rows:]):
        high, low = split(part)
        results.append(mm(left[0], high) + mm(left[0], low) + mm(left[1], high))
    return results


def quarters(value):
    return value[:HALF, :HALF], value[:HALF, HALF:], value[HALF:, :HALF], value[HALF:, HALF:]


def grids():
    rows = lax.broadcasted_iota(jnp.int32, (FRAME, FRAME), 0)
    cols = lax.broadcasted_iota(jnp.int32, (FRAME, FRAME), 1)
    return rows, cols


def rolled(value, r, c):
    return pltpu.roll(pltpu.roll(value, r, axis=0), c, axis=1)


def forward_kernel(
    scal, own, right, below, diag, mod, probe, patt, ph, plo, pth, ptl, spec, ratio, q, power, inten
):
    m = pl.program_id(0)

    @pl.when(m == 0)
    def _():
        rows, cols = grids()
        total = jnp.zeros((FRAME, FRAME), F32)
        for s in range(2):
            r, c = scal[2 * s], scal[2 * s + 1]
            parts = []
            for i in range(2):
                top = jnp.where(cols < c, right[i], own[i])
                bottom = jnp.where(cols < c, diag[i], below[i])
                tile = jnp.where(rows < r, bottom, top)
                parts.append(rolled(tile, lax.rem(FRAME - r, FRAME), lax.rem(FRAME - c, FRAME)))
            a, b = parts
            total = total + scal[4 + s].astype(F32) * (a * a + b * b)
            q[s, 0] = a * mod[0] - b * mod[1]
            q[s, 1] = a * mod[1] + b * mod[0]
            inten[s] = jnp.zeros((FRAME, FRAME), F32)
        power[...] = total

    pr, pi = probe[0, 0], probe[1, 0]
    for s in range(2):
        qr, qi = q[s, 0], q[s, 1]
        wr, wi = pr * qr - pi * qi, pr * qi + pi * qr
        mr, mi = two_sided(wr, wi, (ph[...], plo[...]), (pth[...], ptl[...]))
        acc, acs, asc, ass = quarters(mr)
        bcc, bcs, bsc, bss = quarters(mi)
        e1, e2 = acc - ass, acc + ass
        f1, f2 = bcs + bsc, bsc - bcs
        g1, g2 = bcc - bss, bcc + bss
        h1, h2 = acs + asc, acs - asc
        quads = (
            (0, 0, e1 + f1, g1 - h1),
            (0, HALF, e2 + f2, g2 + h2),
            (HALF, 0, e2 - f2, g2 - h2),
            (HALF, HALF, e1 - f1, g1 + h1),
        )
        for y, x, re, im in quads:
            spec[s, 0, 0, pl.ds(y, HALF), pl.ds(x, HALF)] = re
            spec[s, 0, 1, pl.ds(y, HALF), pl.ds(x, HALF)] = im
            inten[s, pl.ds(y, HALF), pl.ds(x, HALF)] += re * re + im * im

    @pl.when(m == MODES - 1)
    def _():
        for s in range(2):
            ratio[s] = patt[s] / jnp.sqrt(jnp.maximum(inten[s], INTENSITY_FLOOR))


def forward(scal, tiles, mod, probe, patt, tabs):
    return pl.pallas_call(
        forward_kernel,
        grid=(MODES,),
        in_specs=[smem()]
        + [full(2, FRAME, FRAME)] * 5
        + [pl.BlockSpec((2, 1, FRAME, FRAME), lambda m: (0, m, 0, 0)), full(2, FRAME, FRAME)]
        + [full(FRAME, FRAME)] * 4,
        out_specs=[
            pl.BlockSpec((2, 1, 2, FRAME, FRAME), lambda m: (0, m, 0, 0, 0)),
            full(2, FRAME, FRAME),
            full(2, 2, FRAME, FRAME),
            full(FRAME, FRAME),
        ],
        out_shape=[
            shape_of(2, MODES, 2, FRAME, FRAME),
            shape_of(2, FRAME, FRAME),
            shape_of(2, 2, FRAME, FRAME),
            shape_of(FRAME, FRAME),
        ],
        scratch_shapes=[pltpu.VMEM((2, FRAME, FRAME), F32)],
        compiler_params=PARAMS,
        name="forward_spectra",
    )(scal, *tiles, mod, probe, patt, *tabs)


def put_tiles(scal, ref, slot, value):
    for t in range(64):
        part, place = t % 16 // 8, t % 8
        where = scal[8 + 4 * part + t // 16]
        i, j = t // 2, t % 2
        ref[slot, part, where, place, 0] = value[8 * i : 8 * i + 8, HALF * j : HALF * j + HALF]


def inverse_kernel(count, scal, spec, ratio, q, probe, power, ph, plo, pth, ptl, grad, numer):
    m = pl.program_id(0)

    @pl.when(m == 0)
    def _():
        numer[...] = jnp.zeros_like(numer)

    def one_mode():
        pr, pi = probe[0, 0], probe[1, 0]
        gr = jnp.zeros((FRAME, FRAME), F32)
        gi = jnp.zeros((FRAME, FRAME), F32)
        for s in range(2):
            live = scal[4 + s].astype(F32)
            rq = quarters(ratio[s])
            re = [a * b for a, b in zip(quarters(spec[s, 0, 0]), rq)]
            im = [a * b for a, b in zip(quarters(spec[s, 0, 1]), rq)]
            s1r, d1r, s2r, d2r = re[0] + re[3], re[0] - re[3], re[1] + re[2], re[1] - re[2]
            s1i, d1i, s2i, d2i = im[0] + im[3], im[3] - im[0], im[1] + im[2], im[1] - im[2]
            join = lambda a, b, axis: jnp.concatenate([a, b], axis=axis)
            ur = join(join(s1r + s2r, d1i + d2i, 1), join(d1i - d2i, s2r - s1r, 1), 0)
            ui = join(join(s1i + s2i, d1r - d2r, 1), join(d1r + d2r, s2i - s1i, 1), 0)
            nr, ni = two_sided(ur, ui, (pth[...], ptl[...]), (ph[...], plo[...]))
            qr, qi = q[s, 0], q[s, 1]
            dr = (nr - (pr * qr - pi * qi)) * live
            di = (ni - (pr * qi + pi * qr)) * live
            numer[s, 0] += pr * dr + pi * di
            numer[s, 1] += pr * di - pi * dr
            gr = gr + (qr * dr + qi * di)
            gi = gi + (qr * di - qi * dr)
        put_tiles(scal, grad, scal[6], gr)
        put_tiles(scal, grad, scal[7], gi)

    if power is None:
        one_mode()
    else:
        pl.when(m < count)(one_mode)

        @pl.when(m == count)
        def _():
            put_tiles(scal, grad, 0, power[...])
            put_tiles(scal, grad, 1, power[...])


def inverse(scal, spec, ratio, q, probe, power, tabs, first, count):
    planes = count if power is None else count + 1
    last = first + count - 1
    mode = lambda m: jnp.minimum(m + first, last)
    if power is None:
        body = lambda *refs: inverse_kernel(count, *refs[:5], None, *refs[5:])
    else:
        body = lambda *refs: inverse_kernel(count, *refs)
    return pl.pallas_call(
        body,
        grid=(planes,),
        in_specs=[
            smem(),
            pl.BlockSpec((2, 1, 2, FRAME, FRAME), lambda m: (0, mode(m), 0, 0, 0)),
            full(2, FRAME, FRAME),
            full(2, 2, FRAME, FRAME),
            pl.BlockSpec((2, 1, FRAME, FRAME), lambda m: (0, mode(m), 0, 0)),
        ]
        + ([] if power is None else [full(FRAME, FRAME)])
        + [full(FRAME, FRAME)] * 4,
        out_specs=[
            pl.BlockSpec((2, 2, 4, 8, 1, 8, HALF), lambda m: (0, 0, 0, 0, m, 0, 0)),
            full(2, 2, FRAME, FRAME),
        ],
        out_shape=[shape_of(2, 2, 4, 8, planes, 8, HALF), shape_of(2, 2, FRAME, FRAME)],
        compiler_params=PARAMS,
        name=f"inverse_updates_{first}",
    )(scal, spec, ratio, q, probe, *([] if power is None else [power]), *tabs)


def light_kernel(scal, left, up, corner, probe, light):
    power = jnp.zeros((FRAME, FRAME), F32)
    for m in range(MODES):
        power = power + (probe[0, m] * probe[0, m] + probe[1, m] * probe[1, m])
    rows, cols = grids()
    total = jnp.zeros((FRAME, FRAME), F32)
    for source, low_row, low_col in ((scal, 0, 0), (left, 0, 1), (up, 1, 0), (corner, 1, 1)):
        for s in range(2):
            r, c = source[2 * s], source[2 * s + 1]
            keep = ((rows < r) if low_row else (rows >= r)) & ((cols < c) if low_col else (cols >= c))
            moved = source[4 + s].astype(F32) * rolled(power, r, c)
            total = total + jnp.where(keep, moved, 0.0)
    light[...] = total


def light_of(scal, left, up, corner, probe):
    return pl.pallas_call(
        light_kernel,
        in_specs=[smem()] * 4 + [vmem()],
        out_specs=vmem(),
        out_shape=shape_of(FRAME, FRAME),
        compiler_params=PARAMS,
        name="illumination",
    )(scal, left, up, corner, probe)


def place_kernel(scal, first, second, mod, out):
    rows, cols = grids()
    pieces = []
    for s in range(2):
        r, c = scal[2 * s], scal[2 * s + 1]
        a, b = first[s, 0] + second[s, 0], first[s, 1] + second[s, 1]
        real = rolled(a * mod[0] + b * mod[1], r, c)
        imag = rolled(b * mod[0] - a * mod[1], r, c)
        pieces.append((rows < r, cols < c, (real, imag)))
    for tile in range(4):
        for i in range(2):
            total = jnp.zeros((FRAME, FRAME), F32)
            for low_row, low_col, values in pieces:
                keep = (low_row if tile // 2 else ~low_row) & (low_col if tile % 2 else ~low_col)
                total = total + jnp.where(keep, values[i], 0.0)
            out[tile, i] = total


def place(scal, first, second, mod):
    return pl.pallas_call(
        place_kernel,
        in_specs=[smem()] + [vmem()] * 3,
        out_specs=vmem(),
        out_shape=shape_of(4, 2, FRAME, FRAME),
        compiler_params=PARAMS,
        name="place_numerator",
    )(scal, first, second, mod)


def update_kernel(field, own, above, left, light, out, edges):
    inverse_light = 1.0 / (light[...] + OBJECT_DELTA)
    for i in range(2):
        value = field[i] + (own[0, i] + above[0, i] + left[i]) * inverse_light
        out[i] = value
        edges[0, i] = value[0]
        edges[1, i] = value[FRAME - 1]
        edges[2, i] = value[:, :HALF].T[0]
        edges[3, i] = value[:, HALF:].T[HALF - 1]


def update(field, own, above, left, light):
    return pl.pallas_call(
        update_kernel,
        in_specs=[vmem()] * 5,
        out_specs=[vmem()] * 2,
        out_shape=[shape_of(2, FRAME, FRAME), shape_of(4, 2, FRAME)],
        compiler_params=PARAMS,
        name="update_object",
    )(field, own, above, left, light)


def smooth_kernel(field, above, below, left, right, out):
    rows, cols = grids()
    for i in range(2):
        value = field[i]
        column = lambda ref: jnp.broadcast_to(ref[i][None, :], (HALF, FRAME)).T
        wide = lambda ref: jnp.concatenate([column(ref), column(ref)], axis=1)
        north = jnp.where(rows == 0, above[i][None, :], pltpu.roll(value, 1, axis=0))
        south = jnp.where(rows == FRAME - 1, below[i][None, :], pltpu.roll(value, FRAME - 1, axis=0))
        west = jnp.where(cols == 0, wide(left), pltpu.roll(value, 1, axis=1))
        east = jnp.where(cols == FRAME - 1, wide(right), pltpu.roll(value, FRAME - 1, axis=1))
        out[i] = value + SMOOTH_WEIGHT * (north + south + east + west - 4.0 * value)


def smooth(field, above, below, left, right):
    return pl.pallas_call(
        smooth_kernel,
        in_specs=[vmem()] * 5,
        out_specs=vmem(),
        out_shape=shape_of(2, FRAME, FRAME),
        compiler_params=PARAMS,
        name="smooth_object",
    )(field, above, below, left, right)


def gather_kernel(scal, mine, theirs, out):
    for half in range(2):
        for t in range(64):
            part, place_, i, j = t % 16 // 8, t % 8, t // 2, t % 2
            where = scal[8 + 4 * part + t // 16]
            block = (pl.ds(8 * i, 8), pl.ds(HALF * j, HALF))
            if half == 0:
                out[(scal[8 + 8], 0) + block] = mine[part, where, place_, 0]
            else:
                out[(scal[8 + 9], 0) + block] = theirs[part, where, place_, 0]


def gather_probe(scal, mine, theirs):
    piece = pl.BlockSpec((2, 4, 8, 1, 8, HALF), lambda m: (0, 0, 0, m, 0, 0))
    return pl.pallas_call(
        gather_kernel,
        grid=(MODES,),
        in_specs=[smem(), piece, piece],
        out_specs=pl.BlockSpec((2, 1, FRAME, FRAME), lambda m: (0, m, 0, 0)),
        out_shape=shape_of(2, MODES, FRAME, FRAME),
        compiler_params=PARAMS,
        name="gather_probe",
    )(scal, mine, theirs)


def shifted(value, axis, steps):
    count = lax.axis_size(axis)
    first, last = (max(0, -steps), min(count, count - steps))
    return lax.ppermute(value, axis, [(source, source + steps) for source in range(first, last)])


def flip_patterns(patterns):
    rows = jnp.concatenate([patterns[:, :HALF], jnp.flip(patterns[:, HALF:], 1)], axis=1)
    return jnp.concatenate([rows[:, :, :HALF], jnp.flip(rows[:, :, HALF:], 2)], axis=2)


def swap_y(value, bits):
    return lax.ppermute(value, "row", [(r, r ^ (2 * bits)) for r in range(8)])


def swap_core(value):
    return lax.ppermute(value, "row", [(r, r ^ 1) for r in range(8)])


def reduce_y(kept, sent):
    total = kept + swap_core(sent)
    first_a = total[0, :2] + swap_y(total[0, 2:], 1)
    first_b = total[1, :2] + swap_y(total[1, 2:], 3)
    second_a = first_a[0] + swap_y(first_a[1], 3)
    second_b = first_b[0] + swap_y(first_b[1], 1)
    return second_a, second_b


def spread_y(piece):
    a, b = piece[:8], piece[8:]
    pair_a = jnp.stack([a, swap_y(a, 3)])
    pair_b = jnp.stack([b, swap_y(b, 1)])
    four_a = jnp.concatenate([pair_a, swap_y(pair_a, 1)])
    four_b = jnp.concatenate([pair_b, swap_y(pair_b, 3)])
    return jnp.stack([four_a, four_b])


def per_device(object_field, probe_modes, patterns, offsets, counts):
    tabs, mod = tables()
    row, col = lax.axis_index("row"), lax.axis_index("col")
    y, core = row // 2, row % 2
    live = (jnp.arange(2) < counts[0]).astype(jnp.int32)
    r = offsets[0] - row * FRAME
    c = offsets[1] - col * FRAME
    order_a = jnp.array([0, 2, 3, 1], jnp.int32)
    order_b = jnp.array([0, 1, 3, 2], jnp.int32)
    quarter = jnp.bitwise_xor(jnp.arange(4), y)
    places = jnp.stack([r[0], c[0], r[1], c[1], live[0], live[1], core, 1 - core])
    scal = jnp.concatenate(
        [places, order_a[quarter], order_b[quarter], jnp.stack([core, 1 - core])]
    ).astype(jnp.int32)

    right = shifted(object_field, "col", -1)
    below = shifted(object_field, "row", -1)
    diag = shifted(right, "row", -1)
    from_left = shifted(scal, "col", 1)
    from_up = shifted(scal, "row", 1)
    from_corner = shifted(from_left, "row", 1)
    light = light_of(scal, from_left, from_up, from_corner, probe_modes)
    patt = flip_patterns(patterns)

    spec, ratio, q, power = forward(
        scal, (object_field, right, below, diag), mod, probe_modes, patt, tabs
    )
    grad_1, numer_1 = inverse(scal, spec, ratio, q, probe_modes, power, tabs, 0, 4)
    grad_2, numer_2 = inverse(scal, spec, ratio, q, probe_modes, None, tabs, 4, 4)

    one_a, one_b = reduce_y(grad_1[0], grad_1[1])
    two_a, two_b = reduce_y(grad_2[0], grad_2[1])
    mine = jnp.concatenate(
        [jnp.concatenate([one_a, two_a], axis=1), jnp.concatenate([one_b, two_b], axis=1)], axis=0
    )
    sums = jnp.sum(lax.all_to_all(mine, "col", split_axis=0, concat_axis=0, tiled=True), axis=0)
    gradient = jnp.concatenate([sums[:4], sums[5:]], axis=0)
    tile = y * 16 + col
    old = lax.dynamic_slice(
        probe_modes, (core, 0, tile // 2 * 8, tile % 2 * HALF), (1, MODES, 8, HALF)
    )[0]
    fresh = old + gradient / (sums[4] + PROBE_DELTA)
    spread = jnp.broadcast_to(fresh[None], (16,) + fresh.shape)
    piece = lax.all_to_all(spread, "col", split_axis=0, concat_axis=0, tiled=True)
    all_mine = spread_y(piece)
    new_probe = gather_probe(scal, all_mine, swap_core(all_mine))

    tiles = place(scal, numer_1, numer_2, mod)
    above = shifted(tiles[2:], "row", 1)
    from_side = shifted(tiles[1] + above[1], "col", 1)
    updated, edges = update(object_field, tiles, above, from_side, light)
    new_object = smooth(
        updated,
        shifted(edges[1], "row", 1),
        shifted(edges[0], "row", -1),
        shifted(edges[3], "col", 1),
        shifted(edges[2], "col", -1),
    )
    return (new_object, new_probe)


def solution(mesh):
    return jax.shard_map(
        per_device,
        mesh=mesh,
        in_specs=(
            P(None, "row", "col"),
            P(),
            P(("row", "col"), None, None),
            P(None, ("row", "col")),
            P(("row", "col")),
        ),
        out_specs=(P(None, "row", "col"), P()),
        check_vma=False,
    )
```

```python
import math

import jax
import jax.numpy as jnp
import numpy as np
from jax import lax
from jax.experimental import pallas as pl
from jax.experimental.pallas import tpu as pltpu
from jax.sharding import PartitionSpec as P

INTENSITY_FLOOR = 0.1
OBJECT_DELTA = 0.5
PROBE_DELTA = 1.0
SMOOTH_WEIGHT = 0.1
FRAME = 256
HALF = 128
MODES = 8
F32 = jnp.float32
BF16 = jnp.bfloat16
PARAMS = pltpu.CompilerParams(vmem_limit_bytes=58 * 1024 * 1024)


def tables():
    k = np.arange(HALF)[:, None] + 0.5
    x = np.arange(FRAME)[None, :]
    angle = 2.0 * math.pi * k * x / FRAME
    packed = np.concatenate([np.cos(angle), np.sin(angle)], axis=0) / math.sqrt(FRAME)
    high = packed.astype(np.float32).astype(jnp.bfloat16)
    low = (packed - high.astype(np.float64)).astype(np.float32).astype(jnp.bfloat16)
    ramp = np.arange(FRAME)
    phase = math.pi * (ramp[:, None] + ramp[None, :]) / FRAME
    mod = np.stack([np.cos(phase), np.sin(phase)]).astype(np.float32)
    return (high, low, high.T.copy(), low.T.copy()), mod


def full(*shape):
    return pl.BlockSpec(shape, lambda m: (0,) * len(shape))


def smem():
    return pl.BlockSpec(memory_space=pltpu.SMEM)


def vmem():
    return pl.BlockSpec(memory_space=pltpu.VMEM)


def shape_of(*shape):
    return jax.ShapeDtypeStruct(shape, F32)


def split(value):
    high = value.astype(BF16)
    return high, (value - high.astype(F32)).astype(BF16)


def mm(a, b):
    return jnp.dot(a, b, preferred_element_type=F32)


def two_sided(real, imag, left, right):
    rows = real.shape[0]
    high, low = split(jnp.concatenate([real, imag], axis=0))
    first = mm(high, right[0]) + mm(low, right[0]) + mm(high, right[1])
    results = []
    for part in (first[:rows], first[rows:]):
        high, low = split(part)
        results.append(mm(left[0], high) + mm(left[0], low) + mm(left[1], high))
    return results


def quarters(value):
    return value[:HALF, :HALF], value[:HALF, HALF:], value[HALF:, :HALF], value[HALF:, HALF:]


def grids():
    rows = lax.broadcasted_iota(jnp.int32, (FRAME, FRAME), 0)
    cols = lax.broadcasted_iota(jnp.int32, (FRAME, FRAME), 1)
    return rows, cols


def rolled(value, r, c):
    return pltpu.roll(pltpu.roll(value, r, axis=0), c, axis=1)


def spot(offsets, s):
    return offsets[0, s] & (FRAME - 1), offsets[1, s] & (FRAME - 1)


def alive(counts, s):
    return (s < counts[0]).astype(F32)


def forward_kernel(
    offsets, counts, own, right_a, right_b, below, diag_a, diag_b, mod, probe, patt, ph, plo, pth, ptl, spec, ratio, q, power, inten
):
    m = pl.program_id(0)

    @pl.when(m == 0)
    def _():
        rows, cols = grids()
        total = jnp.zeros((FRAME, FRAME), F32)
        for s in range(2):
            r, c = spot(offsets, s)
            parts = []
            for i in range(2):
                right = jnp.concatenate([right_a[i], right_b[i]], axis=0)
                diag = jnp.concatenate([diag_a[i], diag_b[i]], axis=0)
                top = jnp.where(cols < c, right, own[i])
                bottom = jnp.where(cols < c, diag, below[i])
                tile = jnp.where(rows < r, bottom, top)
                parts.append(rolled(tile, lax.rem(FRAME - r, FRAME), lax.rem(FRAME - c, FRAME)))
            a, b = parts
            total = total + alive(counts, s) * (a * a + b * b)
            q[s, 0] = a * mod[0] - b * mod[1]
            q[s, 1] = a * mod[1] + b * mod[0]
            inten[s] = jnp.zeros((FRAME, FRAME), F32)
        power[...] = total

    pr, pi = probe[0, 0], probe[1, 0]
    for s in range(2):
        qr, qi = q[s, 0], q[s, 1]
        wr, wi = pr * qr - pi * qi, pr * qi + pi * qr
        mr, mi = two_sided(wr, wi, (ph[...], plo[...]), (pth[...], ptl[...]))
        acc, acs, asc, ass = quarters(mr)
        bcc, bcs, bsc, bss = quarters(mi)
        e1, e2 = acc - ass, acc + ass
        f1, f2 = bcs + bsc, bsc - bcs
        g1, g2 = bcc - bss, bcc + bss
        h1, h2 = acs + asc, acs - asc
        quads = (
            (0, 0, e1 + f1, g1 - h1),
            (0, HALF, e2 + f2, g2 + h2),
            (HALF, 0, e2 - f2, g2 - h2),
            (HALF, HALF, e1 - f1, g1 + h1),
        )
        for y, x, re, im in quads:
            spec[s, 0, 0, pl.ds(y, HALF), pl.ds(x, HALF)] = re
            spec[s, 0, 1, pl.ds(y, HALF), pl.ds(x, HALF)] = im
            inten[s, pl.ds(y, HALF), pl.ds(x, HALF)] += re * re + im * im

    @pl.when(m == MODES - 1)
    def _():
        for s in range(2):
            ratio[s] = patt[s] / jnp.sqrt(jnp.maximum(inten[s], INTENSITY_FLOOR))


def forward(offsets, counts, tiles, mod, probe, patt, tabs):
    return pl.pallas_call(
        forward_kernel,
        grid=(MODES,),
        in_specs=[smem()] * 2
        + [full(2, FRAME, FRAME)]
        + [full(2, HALF, FRAME)] * 2
        + [full(2, FRAME, FRAME)]
        + [full(2, HALF, FRAME)] * 2
        + [full(2, FRAME, FRAME)]
        + [pl.BlockSpec((2, 1, FRAME, FRAME), lambda m: (0, m, 0, 0)), full(2, FRAME, FRAME)]
        + [full(FRAME, FRAME)] * 4,
        out_specs=[
            pl.BlockSpec((2, 1, 2, FRAME, FRAME), lambda m: (0, m, 0, 0, 0)),
            full(2, FRAME, FRAME),
            full(2, 2, FRAME, FRAME),
            full(FRAME, FRAME),
        ],
        out_shape=[
            shape_of(2, MODES, 2, FRAME, FRAME),
            shape_of(2, FRAME, FRAME),
            shape_of(2, 2, FRAME, FRAME),
            shape_of(FRAME, FRAME),
        ],
        scratch_shapes=[pltpu.VMEM((2, FRAME, FRAME), F32)],
        compiler_params=PARAMS,
    )(offsets, counts, *tiles, mod, probe, patt, *tabs)


def quarter_place(row, part, t):
    v = (t // 16) ^ (row[0] // 2)
    if part == 1:
        return v ^ (v >> 1)
    return jnp.where(v == 0, 0, jnp.where(v == 3, 1, v + 1))


def put_tiles(row, ref, value):
    for t in range(64):
        part, place = t % 16 // 8, t % 8
        where = quarter_place(row, part, t)
        i, j = t // 2, t % 2
        ref[part, where, place, 0] = value[8 * i : 8 * i + 8, HALF * j : HALF * j + HALF]


def inverse_kernel(count, row, counts, spec, ratio, q, probe, power, ph, plo, pth, ptl, kept, sent, numer):
    m = pl.program_id(0)

    @pl.when(m == 0)
    def _():
        numer[...] = jnp.zeros_like(numer)

    def one_mode():
        pr, pi = probe[0, 0], probe[1, 0]
        gr = jnp.zeros((FRAME, FRAME), F32)
        gi = jnp.zeros((FRAME, FRAME), F32)
        for s in range(2):
            live = alive(counts, s)
            rq = quarters(ratio[s])
            re = [a * b for a, b in zip(quarters(spec[s, 0, 0]), rq)]
            im = [a * b for a, b in zip(quarters(spec[s, 0, 1]), rq)]
            s1r, d1r, s2r, d2r = re[0] + re[3], re[0] - re[3], re[1] + re[2], re[1] - re[2]
            s1i, d1i, s2i, d2i = im[0] + im[3], im[3] - im[0], im[1] + im[2], im[1] - im[2]
            join = lambda a, b, axis: jnp.concatenate([a, b], axis=axis)
            ur = join(join(s1r + s2r, d1i + d2i, 1), join(d1i - d2i, s2r - s1r, 1), 0)
            ui = join(join(s1i + s2i, d1r - d2r, 1), join(d1r + d2r, s2i - s1i, 1), 0)
            nr, ni = two_sided(ur, ui, (pth[...], ptl[...]), (ph[...], plo[...]))
            qr, qi = q[s, 0], q[s, 1]
            dr = (nr - (pr * qr - pi * qi)) * live
            di = (ni - (pr * qi + pi * qr)) * live
            numer[s, 0] += pr * dr + pi * di
            numer[s, 1] += pr * di - pi * dr
            gr = gr + (qr * dr + qi * di)
            gi = gi + (qr * di - qi * dr)
        first_core = row[0] % 2 == 0
        put_tiles(row, kept, jnp.where(first_core, gr, gi))
        put_tiles(row, sent, jnp.where(first_core, gi, gr))

    if power is None:
        one_mode()
    else:
        pl.when(m < count)(one_mode)

        @pl.when(m == count)
        def _():
            put_tiles(row, kept, power[...])
            put_tiles(row, sent, power[...])


def inverse(row, counts, spec, ratio, q, probe, power, tabs, first, count):
    planes = count if power is None else count + 1
    last = first + count - 1
    mode = lambda m: jnp.minimum(m + first, last)
    if power is None:
        body = lambda *refs: inverse_kernel(count, *refs[:6], None, *refs[6:])
    else:
        body = lambda *refs: inverse_kernel(count, *refs)
    return pl.pallas_call(
        body,
        grid=(planes,),
        in_specs=[
            smem(),
            smem(),
            pl.BlockSpec((2, 1, 2, FRAME, FRAME), lambda m: (0, mode(m), 0, 0, 0)),
            full(2, FRAME, FRAME),
            full(2, 2, FRAME, FRAME),
            pl.BlockSpec((2, 1, FRAME, FRAME), lambda m: (0, mode(m), 0, 0)),
        ]
        + ([] if power is None else [full(FRAME, FRAME)])
        + [full(FRAME, FRAME)] * 4,
        out_specs=[
            pl.BlockSpec((2, 4, 8, 1, 8, HALF), lambda m: (0, 0, 0, m, 0, 0)),
            pl.BlockSpec((2, 4, 8, 1, 8, HALF), lambda m: (0, 0, 0, m, 0, 0)),
            full(2, 2, FRAME, FRAME),
        ],
        out_shape=[shape_of(2, 4, 8, planes, 8, HALF)] * 2 + [shape_of(2, 2, FRAME, FRAME)],
        compiler_params=PARAMS,
    )(row, counts, spec, ratio, q, probe, *([] if power is None else [power]), *tabs)


def light_kernel(offsets, left, up, corner, probe, light):
    power = jnp.zeros((FRAME, FRAME), F32)
    for m in range(MODES):
        power = power + (probe[0, m] * probe[0, m] + probe[1, m] * probe[1, m])
    rows, cols = grids()
    total = jnp.zeros((FRAME, FRAME), F32)
    for source, low_row, low_col in ((offsets, 0, 0), (left, 0, 1), (up, 1, 0), (corner, 1, 1)):
        for s in range(2):
            r, c = spot(source, s)
            keep = ((rows < r) if low_row else (rows >= r)) & ((cols < c) if low_col else (cols >= c))
            moved = source[2, s].astype(F32) * rolled(power, r, c)
            total = total + jnp.where(keep, moved, 0.0)
    light[...] = total


def light_of(offsets, left, up, corner, probe):
    return pl.pallas_call(
        light_kernel,
        in_specs=[smem()] * 4 + [vmem()],
        out_specs=vmem(),
        out_shape=shape_of(FRAME, FRAME),
        compiler_params=PARAMS,
    )(offsets, left, up, corner, probe)


def place_kernel(offsets, n0, n1, n2, mod, low, side, own):
    rows, cols = grids()
    pieces = []
    for s in range(2):
        r, c = spot(offsets, s)
        a, b = (n0[s, i] + n1[s, i] + n2[s, i] for i in range(2))
        real = rolled(a * mod[0] + b * mod[1], r, c)
        imag = rolled(b * mod[0] - a * mod[1], r, c)
        pieces.append((rows < r, cols < c, (real, imag)))
    for tile, out in ((2, low.at[0]), (3, low.at[1]), (1, side), (0, own)):
        for i in range(2):
            total = jnp.zeros((FRAME, FRAME), F32)
            for low_row, low_col, values in pieces:
                keep = (low_row if tile // 2 else ~low_row) & (low_col if tile % 2 else ~low_col)
                total = total + jnp.where(keep, values[i], 0.0)
            out[i] = total


def place(offsets, numers, mod):
    return pl.pallas_call(
        place_kernel,
        in_specs=[smem()] + [vmem()] * 4,
        out_specs=[vmem()] * 3,
        out_shape=[shape_of(2, 2, FRAME, FRAME)] + [shape_of(2, FRAME, FRAME)] * 2,
        compiler_params=PARAMS,
    )(offsets, *numers, mod)


def update_kernel(field, own, above, left, light, out, edges):
    inverse_light = 1.0 / (light[...] + OBJECT_DELTA)
    for i in range(2):
        value = field[i] + (own[i] + above[0, i] + left[i]) * inverse_light
        out[i] = value
        edges[0, i] = value[0]
        edges[1, i] = value[FRAME - 1]
        edges[2, i] = value[:, :HALF].T[0]
        edges[3, i] = value[:, HALF:].T[HALF - 1]


def update(field, own, above, left, light):
    return pl.pallas_call(
        update_kernel,
        in_specs=[vmem()] * 5,
        out_specs=[vmem()] * 2,
        out_shape=[shape_of(2, FRAME, FRAME), shape_of(4, 2, FRAME)],
        compiler_params=PARAMS,
    )(field, own, above, left, light)


def smooth_kernel(field, above, below, left, right, out):
    rows, cols = grids()
    for i in range(2):
        value = field[i]
        column = lambda ref: jnp.broadcast_to(ref[i][None, :], (HALF, FRAME)).T
        wide = lambda ref: jnp.concatenate([column(ref), column(ref)], axis=1)
        north = jnp.where(rows == 0, above[i][None, :], pltpu.roll(value, 1, axis=0))
        south = jnp.where(rows == FRAME - 1, below[i][None, :], pltpu.roll(value, FRAME - 1, axis=0))
        west = jnp.where(cols == 0, wide(left), pltpu.roll(value, 1, axis=1))
        east = jnp.where(cols == FRAME - 1, wide(right), pltpu.roll(value, FRAME - 1, axis=1))
        out[i] = value + SMOOTH_WEIGHT * (north + south + east + west - 4.0 * value)


def smooth(field, above, below, left, right):
    return pl.pallas_call(
        smooth_kernel,
        in_specs=[vmem()] * 5,
        out_specs=vmem(),
        out_shape=shape_of(2, FRAME, FRAME),
        compiler_params=PARAMS,
    )(field, above, below, left, right)


def gather_kernel(other, row, piece, *refs):
    out, buffer, sem = refs[-3:]
    copies = []
    for m in range(MODES):
        for t in range(64):
            part, spot, i, j = t % 16 // 8, t % 8, t // 2, t % 2
            where = quarter_place(row, part, t)
            buffer[m, 8 * i : 8 * i + 8, HALF * j : HALF * j + HALF] = piece[part, where, spot, m]
        copy = pltpu.make_async_copy(buffer.at[m], out.at[(row[0] + other) % 2, m], sem.at[m])
        copy.start()
        copies.append(copy)
    for copy in copies:
        copy.wait()


def gather_half(row, piece, other, target=None):
    anywhere = pl.BlockSpec(memory_space=pl.ANY)
    return pl.pallas_call(
        lambda *refs: gather_kernel(other, *refs),
        in_specs=[smem(), vmem()] + ([] if target is None else [anywhere]),
        out_specs=anywhere,
        out_shape=shape_of(2, MODES, FRAME, FRAME),
        scratch_shapes=[
            pltpu.VMEM((MODES, FRAME, FRAME), F32),
            pltpu.SemaphoreType.DMA((MODES,)),
        ],
        input_output_aliases={} if target is None else {2: 0},
        compiler_params=PARAMS,
    )(row, piece, *([] if target is None else [target]))


def shifted(value, axis, steps):
    count = lax.axis_size(axis)
    first, last = (max(0, -steps), min(count, count - steps))
    return lax.ppermute(value, axis, [(source, source + steps) for source in range(first, last)])


def flip_patterns(patterns):
    rows = jnp.concatenate([patterns[:, :HALF], jnp.flip(patterns[:, HALF:], 1)], axis=1)
    return jnp.concatenate([rows[:, :, :HALF], jnp.flip(rows[:, :, HALF:], 2)], axis=2)


def swap_y(value, bits):
    return lax.ppermute(value, "row", [(r, r ^ (2 * bits)) for r in range(8)])


def swap_core(value):
    return lax.ppermute(value, "row", [(r, r ^ 1) for r in range(8)])


def spread_y(piece):
    a, b = piece[:8], piece[8:]
    pair_a = jnp.stack([a, swap_y(a, 3)])
    pair_b = jnp.stack([b, swap_y(b, 1)])
    last_a = swap_y(pair_a, 1)
    last_b = swap_y(pair_b, 3)
    return jnp.stack([jnp.concatenate([pair_a, last_a]), jnp.concatenate([pair_b, last_b])])


def per_device(object_field, probe_modes, patterns, offsets, counts):
    tabs, mod = tables()
    row_index, col = lax.axis_index("row"), lax.axis_index("col")
    y, core = row_index // 2, row_index % 2
    row = row_index[None]
    live = (lax.broadcasted_iota(jnp.int32, (3, 2), 1) < counts[0]).astype(jnp.int32)
    kind = lax.broadcasted_iota(jnp.int32, (3, 2), 0)
    slots = jnp.where(kind == 2, live, jnp.pad(offsets, ((0, 1), (0, 0))))

    right_a = shifted(object_field[:, :HALF], "col", -1)
    right_b = shifted(object_field[:, HALF:], "col", -1)
    below = shifted(object_field, "row", -1)
    diag_a = shifted(right_a, "row", -1)
    diag_b = shifted(right_b, "row", -1)
    from_left = shifted(slots, "col", 1)
    from_up = shifted(slots, "row", 1)
    corner_pairs = [
        (r * 16 + c, r * 16 + c + 17) for r in range(7) for c in range(15)
    ]
    from_corner = lax.ppermute(slots, ("row", "col"), corner_pairs)
    patt = flip_patterns(patterns)

    tiles = (object_field, right_a, right_b, below, diag_a, diag_b)
    spec, ratio, q, power = forward(offsets, counts, tiles, mod, probe_modes, patt, tabs)
    common = (row, counts, spec, ratio, q, probe_modes)
    kept_a, sent_a, numer_a = inverse(*common, power, tabs, 0, 4)
    other_a = swap_core(sent_a)
    kept_b, sent_b, numer_b = inverse(*common, None, tabs, 4, 2)
    other_b = swap_core(sent_b)
    total_a = jnp.add(kept_a, other_a)
    y1_a = [swap_y(total_a[0, 2:], 1), swap_y(total_a[1, 2:], 3)]
    kept_c, sent_c, numer_c = inverse(*common, None, tabs, 6, 2)
    other_c = swap_core(sent_c)
    low, side, own = place(offsets, (numer_a, numer_b, numer_c), mod)
    total_c = jnp.concatenate([kept_b + other_b, kept_c + other_c], axis=3)
    y1_c = [swap_y(total_c[0, 2:], 1), swap_y(total_c[1, 2:], 3)]
    done_a = [jnp.add(total_a[i, :2], y1_a[i]) for i in range(2)]
    y2_a = [swap_y(done_a[0][1], 3), swap_y(done_a[1][1], 1)]
    done_c = [jnp.add(total_c[i, :2], y1_c[i]) for i in range(2)]
    y2_c = [swap_y(done_c[0][1], 3), swap_y(done_c[1][1], 1)]
    above = shifted(low, "row", 1)
    mine = jnp.concatenate(
        [
            jnp.concatenate([done_a[i][0] + y2_a[i], done_c[i][0] + y2_c[i]], axis=1)
            for i in range(2)
        ],
        axis=0,
    )
    exchange = lambda value: lax.all_to_all(value, "col", split_axis=0, concat_axis=0, tiled=True)
    parts = exchange(mine)
    sums = jnp.sum(parts, axis=0)
    gradient = jnp.concatenate([sums[:4], sums[5:]], axis=0)
    tile = y * 16 + col
    old = lax.dynamic_slice(
        probe_modes, (core, 0, tile // 2 * 8, tile % 2 * HALF), (1, MODES, 8, HALF)
    )[0]
    fresh = old + gradient / (sums[4] + PROBE_DELTA)
    spread = jnp.broadcast_to(fresh[None], (16,) + fresh.shape)
    from_side = shifted(side + above[1], "col", 1)
    piece = exchange(spread)
    all_mine = spread_y(piece)
    theirs = swap_core(all_mine)
    light = light_of(slots, from_left, from_up, from_corner, probe_modes)
    updated, edges = update(object_field, own, above, from_side, light)
    new_object = smooth(
        updated,
        shifted(edges[1], "row", 1),
        shifted(edges[0], "row", -1),
        shifted(edges[3], "col", 1),
        shifted(edges[2], "col", -1),
    )
    half_probe = gather_half(row, all_mine, 0)
    new_probe = gather_half(row, theirs, 1, half_probe)
    return (new_object, new_probe)


def solution(mesh):
    return jax.shard_map(
        per_device,
        mesh=mesh,
        in_specs=(
            P(None, "row", "col"),
            P(),
            P(("row", "col"), None, None),
            P(None, ("row", "col")),
            P(("row", "col")),
        ),
        out_specs=(P(None, "row", "col"), P()),
        check_vma=False,
    )
```

```python
import math

import jax
import jax.numpy as jnp
import numpy as np
from jax import lax
from jax.experimental import pallas as pl
from jax.experimental.pallas import tpu as pltpu
from jax.sharding import PartitionSpec as P

INTENSITY_FLOOR = 0.1
OBJECT_DELTA = 0.5
PROBE_DELTA = 1.0
SMOOTH_WEIGHT = 0.1
FRAME = 256
HALF = 128
MODES = 8
F32 = jnp.float32
BF16 = jnp.bfloat16
PARAMS = pltpu.CompilerParams(vmem_limit_bytes=58 * 1024 * 1024)


def tables():
    k = np.arange(HALF)[:, None] + 0.5
    x = np.arange(FRAME)[None, :]
    angle = 2.0 * math.pi * k * x / FRAME
    packed = np.concatenate([np.cos(angle), np.sin(angle)], axis=0) / math.sqrt(FRAME)
    high = packed.astype(np.float32).astype(jnp.bfloat16)
    low = (packed - high.astype(np.float64)).astype(np.float32).astype(jnp.bfloat16)
    ramp = np.arange(FRAME)
    phase = math.pi * (ramp[:, None] + ramp[None, :]) / FRAME
    mod = np.stack([np.cos(phase), np.sin(phase)]).astype(np.float32)
    return (high, low, high.T.copy(), low.T.copy()), mod


def full(*shape):
    return pl.BlockSpec(shape, lambda m: (0,) * len(shape))


def smem():
    return pl.BlockSpec(memory_space=pltpu.SMEM)


def vmem():
    return pl.BlockSpec(memory_space=pltpu.VMEM)


def shape_of(*shape):
    return jax.ShapeDtypeStruct(shape, F32)


def split(value):
    high = value.astype(BF16)
    return high, (value - high.astype(F32)).astype(BF16)


def mm(a, b):
    return jnp.dot(a, b, preferred_element_type=F32)


def two_sided(real, imag, left, right):
    parts = []
    for value in (real, imag):
        high, low = split(value)
        both = mm(jnp.concatenate([high, low], axis=0), right[0])
        parts.append(both[:FRAME] + both[FRAME:] + mm(high, right[1]))
    results = []
    for part in parts:
        high, low = split(part)
        both = mm(left[0], high)
        results.append(both[:FRAME] + both[FRAME:] + mm(left[1], low))
    return results


def quarters(value):
    return value[:HALF, :HALF], value[:HALF, HALF:], value[HALF:, :HALF], value[HALF:, HALF:]


def grids():
    rows = lax.broadcasted_iota(jnp.int32, (FRAME, FRAME), 0)
    cols = lax.broadcasted_iota(jnp.int32, (FRAME, FRAME), 1)
    return rows, cols


def rolled(value, r, c):
    return pltpu.roll(pltpu.roll(value, r, axis=0), c, axis=1)


def spot(offsets, s):
    return offsets[0, s] & (FRAME - 1), offsets[1, s] & (FRAME - 1)


def alive(counts, s):
    return (s < counts[0]).astype(F32)


def forward_kernel(
    offsets, counts, own, right_a, right_b, below, diag_a, diag_b, mod, probe, patt, ph, plo, pth, ptl, spec, ratio, q, power, inten
):
    m = pl.program_id(0)

    @pl.when(m == 0)
    def _():
        rows, cols = grids()
        total = jnp.zeros((FRAME, FRAME), F32)
        for s in range(2):
            r, c = spot(offsets, s)
            parts = []
            for i in range(2):
                right = jnp.concatenate([right_a[i], right_b[i]], axis=0)
                diag = jnp.concatenate([diag_a[i], diag_b[i]], axis=0)
                top = jnp.where(cols < c, right, own[i])
                bottom = jnp.where(cols < c, diag, below[i])
                tile = jnp.where(rows < r, bottom, top)
                parts.append(rolled(tile, lax.rem(FRAME - r, FRAME), lax.rem(FRAME - c, FRAME)))
            a, b = parts
            total = total + alive(counts, s) * (a * a + b * b)
            q[s, 0] = a * mod[0] - b * mod[1]
            q[s, 1] = a * mod[1] + b * mod[0]
            inten[s] = jnp.zeros((FRAME, FRAME), F32)
        power[...] = total

    pr, pi = probe[0, 0], probe[1, 0]
    for s in range(2):
        qr, qi = q[s, 0], q[s, 1]
        wr, wi = pr * qr - pi * qi, pr * qi + pi * qr
        mr, mi = two_sided(wr, wi, (jnp.concatenate([ph[...], plo[...]], axis=0), ph[...]), (pth[...], ptl[...]))
        acc, acs, asc, ass = quarters(mr)
        bcc, bcs, bsc, bss = quarters(mi)
        e1, e2 = acc - ass, acc + ass
        f1, f2 = bcs + bsc, bsc - bcs
        g1, g2 = bcc - bss, bcc + bss
        h1, h2 = acs + asc, acs - asc
        quads = (
            (0, 0, e1 + f1, g1 - h1),
            (0, HALF, e2 + f2, g2 + h2),
            (HALF, 0, e2 - f2, g2 - h2),
            (HALF, HALF, e1 - f1, g1 + h1),
        )
        for y, x, re, im in quads:
            spec[s, 0, 0, pl.ds(y, HALF), pl.ds(x, HALF)] = re
            spec[s, 0, 1, pl.ds(y, HALF), pl.ds(x, HALF)] = im
            inten[s, pl.ds(y, HALF), pl.ds(x, HALF)] += re * re + im * im

    @pl.when(m == MODES - 1)
    def _():
        for s in range(2):
            ratio[s] = patt[s] / jnp.sqrt(jnp.maximum(inten[s], INTENSITY_FLOOR))


def forward(offsets, counts, tiles, mod, probe, patt, tabs):
    return pl.pallas_call(
        forward_kernel,
        grid=(MODES,),
        in_specs=[smem()] * 2
        + [full(2, FRAME, FRAME)]
        + [full(2, HALF, FRAME)] * 2
        + [full(2, FRAME, FRAME)]
        + [full(2, HALF, FRAME)] * 2
        + [full(2, FRAME, FRAME)]
        + [pl.BlockSpec((2, 1, FRAME, FRAME), lambda m: (0, m, 0, 0)), full(2, FRAME, FRAME)]
        + [full(FRAME, FRAME)] * 4,
        out_specs=[
            pl.BlockSpec((2, 1, 2, FRAME, FRAME), lambda m: (0, m, 0, 0, 0)),
            full(2, FRAME, FRAME),
            full(2, 2, FRAME, FRAME),
            full(FRAME, FRAME),
        ],
        out_shape=[
            shape_of(2, MODES, 2, FRAME, FRAME),
            shape_of(2, FRAME, FRAME),
            shape_of(2, 2, FRAME, FRAME),
            shape_of(FRAME, FRAME),
        ],
        scratch_shapes=[pltpu.VMEM((2, FRAME, FRAME), F32)],
        compiler_params=PARAMS,
    )(offsets, counts, *tiles, mod, probe, patt, *tabs)


def quarter_place(row, part, t):
    v = (t // 16) ^ (row[0] // 2)
    if part == 1:
        return v ^ (v >> 1)
    return jnp.where(v == 0, 0, jnp.where(v == 3, 1, v + 1))


def put_tiles(row, ref, value):
    for t in range(64):
        part, place = t % 16 // 8, t % 8
        where = quarter_place(row, part, t)
        i, j = t // 2, t % 2
        ref[part, where, place, 0] = value[8 * i : 8 * i + 8, HALF * j : HALF * j + HALF]


def inverse_kernel(count, row, counts, spec, ratio, q, probe, power, ph, plo, pth, ptl, kept, sent, numer):
    m = pl.program_id(0)

    @pl.when(m == 0)
    def _():
        numer[...] = jnp.zeros_like(numer)

    def one_mode():
        pr, pi = probe[0, 0], probe[1, 0]
        gr = jnp.zeros((FRAME, FRAME), F32)
        gi = jnp.zeros((FRAME, FRAME), F32)
        for s in range(2):
            live = alive(counts, s)
            rq = quarters(ratio[s])
            re = [a * b for a, b in zip(quarters(spec[s, 0, 0]), rq)]
            im = [a * b for a, b in zip(quarters(spec[s, 0, 1]), rq)]
            s1r, d1r, s2r, d2r = re[0] + re[3], re[0] - re[3], re[1] + re[2], re[1] - re[2]
            s1i, d1i, s2i, d2i = im[0] + im[3], im[3] - im[0], im[1] + im[2], im[1] - im[2]
            join = lambda a, b, axis: jnp.concatenate([a, b], axis=axis)
            ur = join(join(s1r + s2r, d1i + d2i, 1), join(d1i - d2i, s2r - s1r, 1), 0)
            ui = join(join(s1i + s2i, d1r - d2r, 1), join(d1r + d2r, s2i - s1i, 1), 0)
            nr, ni = two_sided(ur, ui, (jnp.concatenate([pth[...], ptl[...]], axis=0), pth[...]), (ph[...], plo[...]))
            qr, qi = q[s, 0], q[s, 1]
            dr = (nr - (pr * qr - pi * qi)) * live
            di = (ni - (pr * qi + pi * qr)) * live
            numer[s, 0] += pr * dr + pi * di
            numer[s, 1] += pr * di - pi * dr
            gr = gr + (qr * dr + qi * di)
            gi = gi + (qr * di - qi * dr)
        first_core = row[0] % 2 == 0
        put_tiles(row, kept, jnp.where(first_core, gr, gi))
        put_tiles(row, sent, jnp.where(first_core, gi, gr))

    if power is None:
        one_mode()
    else:
        pl.when(m < count)(one_mode)

        @pl.when(m == count)
        def _():
            put_tiles(row, kept, power[...])
            put_tiles(row, sent, power[...])


def inverse(row, counts, spec, ratio, q, probe, power, tabs, first, count):
    planes = count if power is None else count + 1
    last = first + count - 1
    mode = lambda m: jnp.minimum(m + first, last)
    if power is None:
        body = lambda *refs: inverse_kernel(count, *refs[:6], None, *refs[6:])
    else:
        body = lambda *refs: inverse_kernel(count, *refs)
    return pl.pallas_call(
        body,
        grid=(planes,),
        in_specs=[
            smem(),
            smem(),
            pl.BlockSpec((2, 1, 2, FRAME, FRAME), lambda m: (0, mode(m), 0, 0, 0)),
            full(2, FRAME, FRAME),
            full(2, 2, FRAME, FRAME),
            pl.BlockSpec((2, 1, FRAME, FRAME), lambda m: (0, mode(m), 0, 0)),
        ]
        + ([] if power is None else [full(FRAME, FRAME)])
        + [full(FRAME, FRAME)] * 4,
        out_specs=[
            pl.BlockSpec((2, 4, 8, 1, 8, HALF), lambda m: (0, 0, 0, m, 0, 0)),
            pl.BlockSpec((2, 4, 8, 1, 8, HALF), lambda m: (0, 0, 0, m, 0, 0)),
            full(2, 2, FRAME, FRAME),
        ],
        out_shape=[shape_of(2, 4, 8, planes, 8, HALF)] * 2 + [shape_of(2, 2, FRAME, FRAME)],
        compiler_params=PARAMS,
    )(row, counts, spec, ratio, q, probe, *([] if power is None else [power]), *tabs)


def light_kernel(offsets, left, up, corner, probe, light):
    power = jnp.zeros((FRAME, FRAME), F32)
    for m in range(MODES):
        power = power + (probe[0, m] * probe[0, m] + probe[1, m] * probe[1, m])
    rows, cols = grids()
    total = jnp.zeros((FRAME, FRAME), F32)
    for source, low_row, low_col in ((offsets, 0, 0), (left, 0, 1), (up, 1, 0), (corner, 1, 1)):
        for s in range(2):
            r, c = spot(source, s)
            keep = ((rows < r) if low_row else (rows >= r)) & ((cols < c) if low_col else (cols >= c))
            moved = source[2, s].astype(F32) * rolled(power, r, c)
            total = total + jnp.where(keep, moved, 0.0)
    light[...] = total


def light_of(offsets, left, up, corner, probe):
    return pl.pallas_call(
        light_kernel,
        in_specs=[smem()] * 4 + [vmem()],
        out_specs=vmem(),
        out_shape=shape_of(FRAME, FRAME),
        compiler_params=PARAMS,
    )(offsets, left, up, corner, probe)


def place_kernel(offsets, n0, n1, n2, mod, low, side, own):
    rows, cols = grids()
    pieces = []
    for s in range(2):
        r, c = spot(offsets, s)
        a, b = (n0[s, i] + n1[s, i] + n2[s, i] for i in range(2))
        real = rolled(a * mod[0] + b * mod[1], r, c)
        imag = rolled(b * mod[0] - a * mod[1], r, c)
        pieces.append((rows < r, cols < c, (real, imag)))
    for tile, out in ((2, low.at[0]), (3, low.at[1]), (1, side), (0, own)):
        for i in range(2):
            total = jnp.zeros((FRAME, FRAME), F32)
            for low_row, low_col, values in pieces:
                keep = (low_row if tile // 2 else ~low_row) & (low_col if tile % 2 else ~low_col)
                total = total + jnp.where(keep, values[i], 0.0)
            out[i] = total


def place(offsets, numers, mod):
    return pl.pallas_call(
        place_kernel,
        in_specs=[smem()] + [vmem()] * 4,
        out_specs=[vmem()] * 3,
        out_shape=[shape_of(2, 2, FRAME, FRAME)] + [shape_of(2, FRAME, FRAME)] * 2,
        compiler_params=PARAMS,
    )(offsets, *numers, mod)


def update_kernel(index, field, own, above, left, light, out, row_1, row_2, col_1, col_2):
    odd_row, odd_col = index[0] % 2 == 1, index[1] % 2 == 1
    inverse_light = 1.0 / (light[...] + OBJECT_DELTA)
    for i in range(2):
        value = field[i] + (own[i] + above[0, i] + left[i]) * inverse_light
        out[i] = value
        top, bottom = value[0], value[FRAME - 1]
        first, last = value[:, :HALF].T[0], value[:, HALF:].T[HALF - 1]
        row_1[i] = jnp.where(odd_row, top, bottom)
        row_2[i] = jnp.where(odd_row, bottom, top)
        col_1[i] = jnp.where(odd_col, first, last)
        col_2[i] = jnp.where(odd_col, last, first)


def update(index, field, own, above, left, light):
    return pl.pallas_call(
        update_kernel,
        in_specs=[smem()] + [vmem()] * 5,
        out_specs=[vmem()] * 5,
        out_shape=[shape_of(2, FRAME, FRAME)] + [shape_of(2, FRAME)] * 4,
        compiler_params=PARAMS,
    )(index, field, own, above, left, light)


def smooth_kernel(index, field, row_1, row_2, col_1, col_2, out):
    odd_row, odd_col = index[0] % 2 == 1, index[1] % 2 == 1
    rows, cols = grids()
    for i in range(2):
        value = field[i]
        above = jnp.where(odd_row, row_1[i], row_2[i])[None, :]
        below = jnp.where(odd_row, row_2[i], row_1[i])[None, :]
        column = lambda edge: jnp.broadcast_to(edge[None, :], (HALF, FRAME)).T
        wide = lambda edge: jnp.concatenate([column(edge), column(edge)], axis=1)
        left = wide(jnp.where(odd_col, col_1[i], col_2[i]))
        right = wide(jnp.where(odd_col, col_2[i], col_1[i]))
        north = jnp.where(rows == 0, above, pltpu.roll(value, 1, axis=0))
        south = jnp.where(rows == FRAME - 1, below, pltpu.roll(value, FRAME - 1, axis=0))
        west = jnp.where(cols == 0, left, pltpu.roll(value, 1, axis=1))
        east = jnp.where(cols == FRAME - 1, right, pltpu.roll(value, FRAME - 1, axis=1))
        out[i] = value + SMOOTH_WEIGHT * (north + south + east + west - 4.0 * value)


def smooth(index, field, *edges):
    return pl.pallas_call(
        smooth_kernel,
        in_specs=[smem()] + [vmem()] * 5,
        out_specs=vmem(),
        out_shape=shape_of(2, FRAME, FRAME),
        compiler_params=PARAMS,
    )(index, field, *edges)


ORDER = ((0, 3, 1, 2), (0, 1, 3, 2))


def gather_kernel(other, half, index, part_a, part_b, *refs):
    out, buffer, sem = refs[-3:]
    target = (index[0] + other) % 2
    copies = []
    for part, piece in ((0, part_a), (1, part_b)):
        for k in range(2):
            for m in range(MODES):
                for place in range(8):
                    i, j = place // 2, place % 2
                    buffer[part, k, m, 8 * i : 8 * i + 8, HALF * j : HALF * j + HALF] = piece[
                        k, place, m
                    ]
            quarter = ORDER[part][2 * half + k] ^ (index[0] // 2)
            rows = pl.ds(pl.multiple_of(64 * quarter + 32 * part, 32), 32)
            copy = pltpu.make_async_copy(
                buffer.at[part, k], out.at[target, :, rows], sem.at[part, k]
            )
            copy.start()
            copies.append(copy)
    for copy in copies:
        copy.wait()


def gather(index, part_a, part_b, other, half, target=None):
    anywhere = pl.BlockSpec(memory_space=pl.ANY)
    return pl.pallas_call(
        lambda *refs: gather_kernel(other, half, *refs),
        in_specs=[smem(), vmem(), vmem()] + ([] if target is None else [anywhere]),
        out_specs=anywhere,
        out_shape=shape_of(2, MODES, FRAME, FRAME),
        scratch_shapes=[
            pltpu.VMEM((2, 2, MODES, 32, FRAME), F32),
            pltpu.SemaphoreType.DMA((2, 2)),
        ],
        input_output_aliases={} if target is None else {3: 0},
        compiler_params=PARAMS,
    )(index, part_a, part_b, *([] if target is None else [target]))


def shifted(value, axis, steps):
    count = lax.axis_size(axis)
    first, last = (max(0, -steps), min(count, count - steps))
    return lax.ppermute(value, axis, [(source, source + steps) for source in range(first, last)])


def flip_patterns(patterns):
    rows = jnp.concatenate([patterns[:, :HALF], jnp.flip(patterns[:, HALF:], 1)], axis=1)
    return jnp.concatenate([rows[:, :, :HALF], jnp.flip(rows[:, :, HALF:], 2)], axis=2)


def swap_y(value, bits):
    return lax.ppermute(value, "row", [(r, r ^ (2 * bits)) for r in range(8)])


def swap_core(value):
    return lax.ppermute(value, "row", [(r, r ^ 1) for r in range(8)])


def per_device(object_field, probe_modes, patterns, offsets, counts):
    tabs, mod = tables()
    row_index, col = lax.axis_index("row"), lax.axis_index("col")
    y, core = row_index // 2, row_index % 2
    row = jnp.where(lax.iota(jnp.int32, 2) == 0, row_index, col)
    live = (lax.broadcasted_iota(jnp.int32, (3, 2), 1) < counts[0]).astype(jnp.int32)
    kind = lax.broadcasted_iota(jnp.int32, (3, 2), 0)
    slots = jnp.where(kind == 2, live, jnp.pad(offsets, ((0, 1), (0, 0))))

    right_a = shifted(object_field[:, :HALF], "col", -1)
    right_b = shifted(object_field[:, HALF:], "col", -1)
    below = shifted(object_field, "row", -1)
    diag_a = shifted(right_a, "row", -1)
    diag_b = shifted(right_b, "row", -1)
    from_left = shifted(slots, "col", 1)
    from_up = shifted(slots, "row", 1)
    corner_pairs = [(r * 16 + c, r * 16 + c + 17) for r in range(7) for c in range(15)]
    from_corner = lax.ppermute(slots, ("row", "col"), corner_pairs)
    patt = flip_patterns(patterns)

    tiles = (object_field, right_a, right_b, below, diag_a, diag_b)
    spec, ratio, q, power = forward(offsets, counts, tiles, mod, probe_modes, patt, tabs)
    common = (row, counts, spec, ratio, q, probe_modes)
    kept_a, sent_a, numer_a = inverse(*common, power, tabs, 0, 4)
    other_a = swap_core(sent_a)
    kept_b, sent_b, numer_b = inverse(*common, None, tabs, 4, 2)
    other_b = swap_core(sent_b)
    total_a = jnp.add(kept_a, other_a)
    y1_a = [swap_y(total_a[0, 2:], 1), swap_y(total_a[1, 2:], 3)]
    kept_c, sent_c, numer_c = inverse(*common, None, tabs, 6, 2)
    other_c = swap_core(sent_c)
    low, side, own = place(offsets, (numer_a, numer_b, numer_c), mod)
    total_c = jnp.concatenate([kept_b + other_b, kept_c + other_c], axis=3)
    y1_c = [swap_y(total_c[0, 2:], 1), swap_y(total_c[1, 2:], 3)]
    done_a = [jnp.add(total_a[i, :2], y1_a[i]) for i in range(2)]
    y2_a = [swap_y(done_a[0][1], 3), swap_y(done_a[1][1], 1)]
    done_c = [jnp.add(total_c[i, :2], y1_c[i]) for i in range(2)]
    y2_c = [swap_y(done_c[0][1], 3), swap_y(done_c[1][1], 1)]
    above = shifted(low, "row", 1)
    mine = jnp.concatenate(
        [
            jnp.concatenate([done_a[i][0] + y2_a[i], done_c[i][0] + y2_c[i]], axis=1)
            for i in range(2)
        ],
        axis=0,
    )
    exchange = lambda value: lax.all_to_all(value, "col", split_axis=0, concat_axis=0, tiled=True)
    parts = exchange(mine)
    sums = jnp.sum(parts, axis=0)
    gradient = jnp.concatenate([sums[:4], sums[5:]], axis=0)
    tile = y * 16 + col
    old = lax.dynamic_slice(
        probe_modes, (core, 0, tile // 2 * 8, tile % 2 * HALF), (1, MODES, 8, HALF)
    )[0]
    fresh = old + gradient / (sums[4] + PROBE_DELTA)
    spread = jnp.broadcast_to(fresh[None], (16,) + fresh.shape)
    from_side = shifted(side + above[1], "col", 1)
    piece = exchange(spread)
    a, b = piece[:8], piece[8:]
    pair_a = jnp.stack([a, swap_y(a, 3)])
    pair_b = jnp.stack([b, swap_y(b, 1)])
    last_a = swap_y(pair_a, 1)
    last_b = swap_y(pair_b, 3)
    far_a, far_b = swap_core(pair_a), swap_core(pair_b)
    end_a, end_b = swap_core(last_a), swap_core(last_b)
    probe_1 = gather(row, pair_a, pair_b, 0, 0)
    probe_2 = gather(row, far_a, far_b, 1, 0, probe_1)
    probe_3 = gather(row, last_a, last_b, 0, 1, probe_2)
    new_probe = gather(row, end_a, end_b, 1, 1, probe_3)

    light = light_of(slots, from_left, from_up, from_corner, probe_modes)
    updated, *edges = update(row, object_field, own, above, from_side, light)
    between = lambda count: [(i, i ^ 1) for i in range(count)]
    across = lambda count: [(i, ((i + 1) ^ 1) - 1) for i in range(1, count - 1)]
    arrived = [
        lax.ppermute(edges[0], "row", between(8)),
        lax.ppermute(edges[1], "row", across(8)),
        lax.ppermute(edges[2], "col", between(16)),
        lax.ppermute(edges[3], "col", across(16)),
    ]
    new_object = smooth(row, updated, *arrived)
    return (new_object, new_probe)


def solution(mesh):
    return jax.shard_map(
        per_device,
        mesh=mesh,
        in_specs=(
            P(None, "row", "col"),
            P(),
            P(("row", "col"), None, None),
            P(None, ("row", "col")),
            P(("row", "col")),
        ),
        out_specs=(P(None, "row", "col"), P()),
        check_vma=False,
    )
```

```python
import math

import jax
import jax.numpy as jnp
import numpy as np
from jax import lax
from jax.experimental import pallas as pl
from jax.experimental.pallas import tpu as pltpu
from jax.sharding import PartitionSpec as P

INTENSITY_FLOOR = 0.1
OBJECT_DELTA = 0.5
PROBE_DELTA = 1.0
SMOOTH_WEIGHT = 0.1
FRAME = 256
HALF = 128
MODES = 8
F32 = jnp.float32
BF16 = jnp.bfloat16
PARAMS = pltpu.CompilerParams(vmem_limit_bytes=58 * 1024 * 1024)


def tables():
    k = np.arange(HALF)[:, None] + 0.5
    x = np.arange(FRAME)[None, :]
    angle = 2.0 * math.pi * k * x / FRAME
    packed = np.concatenate([np.cos(angle), np.sin(angle)], axis=0) / math.sqrt(FRAME)
    high = packed.astype(np.float32).astype(jnp.bfloat16)
    low = (packed - high.astype(np.float64)).astype(np.float32).astype(jnp.bfloat16)
    ramp = np.arange(FRAME)
    phase = math.pi * (ramp[:, None] + ramp[None, :]) / FRAME
    mod = np.stack([np.cos(phase), np.sin(phase)]).astype(np.float32)
    return (high, low, high.T.copy(), low.T.copy()), mod


def full(*shape):
    return pl.BlockSpec(shape, lambda m: (0,) * len(shape))


def smem():
    return pl.BlockSpec(memory_space=pltpu.SMEM)


def vmem():
    return pl.BlockSpec(memory_space=pltpu.VMEM)


def shape_of(*shape):
    return jax.ShapeDtypeStruct(shape, F32)


def split(value):
    high = value.astype(BF16)
    return high, (value - high.astype(F32)).astype(BF16)


def mm(a, b):
    return jnp.dot(a, b, preferred_element_type=F32)


def two_sided(real, imag, left, right):
    parts = []
    for value in (real, imag):
        high, low = split(value)
        parts.append(mm(high, right[0]) + mm(low, right[0]) + mm(high, right[1]))
    results = []
    for part in parts:
        high, low = split(part)
        both = mm(left[0], high)
        results.append(both[:FRAME] + both[FRAME:] + mm(left[1], low))
    return results


def quarters(value):
    return value[:HALF, :HALF], value[:HALF, HALF:], value[HALF:, :HALF], value[HALF:, HALF:]


def grids():
    rows = lax.broadcasted_iota(jnp.int32, (FRAME, FRAME), 0)
    cols = lax.broadcasted_iota(jnp.int32, (FRAME, FRAME), 1)
    return rows, cols


def rolled(value, r, c):
    return pltpu.roll(pltpu.roll(value, r, axis=0), c, axis=1)


def spot(offsets, s):
    return offsets[0, s] & (FRAME - 1), offsets[1, s] & (FRAME - 1)


def alive(counts, s):
    return (s < counts[0]).astype(F32)


def forward_kernel(
    offsets, counts, own, right_a, right_b, below, diag_a, diag_b, mod, probe, patt, ph, plo, pth, ptl, spec, ratio, q, power, inten
):
    m = pl.program_id(0)

    @pl.when(m == 0)
    def _():
        rows, cols = grids()
        total = jnp.zeros((FRAME, FRAME), F32)
        for s in range(2):
            r, c = spot(offsets, s)
            parts = []
            for i in range(2):
                right = jnp.concatenate([right_a[i], right_b[i]], axis=0)
                diag = jnp.concatenate([diag_a[i], diag_b[i]], axis=0)
                top = jnp.where(cols < c, right, own[i])
                bottom = jnp.where(cols < c, diag, below[i])
                tile = jnp.where(rows < r, bottom, top)
                parts.append(rolled(tile, lax.rem(FRAME - r, FRAME), lax.rem(FRAME - c, FRAME)))
            a, b = parts
            total = total + alive(counts, s) * (a * a + b * b)
            q[s, 0] = a * mod[0] - b * mod[1]
            q[s, 1] = a * mod[1] + b * mod[0]
            inten[s] = jnp.zeros((FRAME, FRAME), F32)
        power[...] = total

    pr, pi = probe[0, 0], probe[1, 0]
    for s in range(2):
        qr, qi = q[s, 0], q[s, 1]
        wr, wi = pr * qr - pi * qi, pr * qi + pi * qr
        mr, mi = two_sided(wr, wi, (jnp.concatenate([ph[...], plo[...]], axis=0), ph[...]), (pth[...], ptl[...]))
        acc, acs, asc, ass = quarters(mr)
        bcc, bcs, bsc, bss = quarters(mi)
        e1, e2 = acc - ass, acc + ass
        f1, f2 = bcs + bsc, bsc - bcs
        g1, g2 = bcc - bss, bcc + bss
        h1, h2 = acs + asc, acs - asc
        quads = (
            (0, 0, e1 + f1, g1 - h1),
            (0, HALF, e2 + f2, g2 + h2),
            (HALF, 0, e2 - f2, g2 - h2),
            (HALF, HALF, e1 - f1, g1 + h1),
        )
        for y, x, re, im in quads:
            spec[s, 0, 0, pl.ds(y, HALF), pl.ds(x, HALF)] = re
            spec[s, 0, 1, pl.ds(y, HALF), pl.ds(x, HALF)] = im
            inten[s, pl.ds(y, HALF), pl.ds(x, HALF)] += re * re + im * im

    @pl.when(m == MODES - 1)
    def _():
        for s in range(2):
            ratio[s] = patt[s] / jnp.sqrt(jnp.maximum(inten[s], INTENSITY_FLOOR))


def forward(offsets, counts, tiles, mod, probe, patt, tabs):
    return pl.pallas_call(
        forward_kernel,
        grid=(MODES,),
        in_specs=[smem()] * 2
        + [full(2, FRAME, FRAME)]
        + [full(2, HALF, FRAME)] * 2
        + [full(2, FRAME, FRAME)]
        + [full(2, HALF, FRAME)] * 2
        + [full(2, FRAME, FRAME)]
        + [pl.BlockSpec((2, 1, FRAME, FRAME), lambda m: (0, m, 0, 0)), full(2, FRAME, FRAME)]
        + [full(FRAME, FRAME)] * 4,
        out_specs=[
            pl.BlockSpec((2, 1, 2, FRAME, FRAME), lambda m: (0, m, 0, 0, 0)),
            full(2, FRAME, FRAME),
            full(2, 2, FRAME, FRAME),
            full(FRAME, FRAME),
        ],
        out_shape=[
            shape_of(2, MODES, 2, FRAME, FRAME),
            shape_of(2, FRAME, FRAME),
            shape_of(2, 2, FRAME, FRAME),
            shape_of(FRAME, FRAME),
        ],
        scratch_shapes=[pltpu.VMEM((2, FRAME, FRAME), F32)],
        compiler_params=PARAMS,
    )(offsets, counts, *tiles, mod, probe, patt, *tabs)


def quarter_place(row, part, t):
    v = (t // 16) ^ (row[0] // 2)
    if part == 1:
        return v ^ (v >> 1)
    return jnp.where(v == 0, 0, jnp.where(v == 3, 1, v + 1))


def put_tiles(row, ref, value):
    for t in range(64):
        part, place = t % 16 // 8, t % 8
        where = quarter_place(row, part, t)
        i, j = t // 2, t % 2
        ref[part, where, place, 0] = value[8 * i : 8 * i + 8, HALF * j : HALF * j + HALF]


def inverse_kernel(count, row, counts, spec, ratio, q, probe, power, ph, plo, pth, ptl, kept, sent, numer):
    m = pl.program_id(0)

    @pl.when(m == 0)
    def _():
        numer[...] = jnp.zeros_like(numer)

    def one_mode():
        pr, pi = probe[0, 0], probe[1, 0]
        gr = jnp.zeros((FRAME, FRAME), F32)
        gi = jnp.zeros((FRAME, FRAME), F32)
        for s in range(2):
            live = alive(counts, s)
            rq = quarters(ratio[s])
            re = [a * b for a, b in zip(quarters(spec[s, 0, 0]), rq)]
            im = [a * b for a, b in zip(quarters(spec[s, 0, 1]), rq)]
            s1r, d1r, s2r, d2r = re[0] + re[3], re[0] - re[3], re[1] + re[2], re[1] - re[2]
            s1i, d1i, s2i, d2i = im[0] + im[3], im[3] - im[0], im[1] + im[2], im[1] - im[2]
            join = lambda a, b, axis: jnp.concatenate([a, b], axis=axis)
            ur = join(join(s1r + s2r, d1i + d2i, 1), join(d1i - d2i, s2r - s1r, 1), 0)
            ui = join(join(s1i + s2i, d1r - d2r, 1), join(d1r + d2r, s2i - s1i, 1), 0)
            nr, ni = two_sided(ur, ui, (jnp.concatenate([pth[...], ptl[...]], axis=0), pth[...]), (ph[...], plo[...]))
            qr, qi = q[s, 0], q[s, 1]
            dr = (nr - (pr * qr - pi * qi)) * live
            di = (ni - (pr * qi + pi * qr)) * live
            numer[s, 0] += pr * dr + pi * di
            numer[s, 1] += pr * di - pi * dr
            gr = gr + (qr * dr + qi * di)
            gi = gi + (qr * di - qi * dr)
        first_core = row[0] % 2 == 0
        put_tiles(row, kept, jnp.where(first_core, gr, gi))
        put_tiles(row, sent, jnp.where(first_core, gi, gr))

    if power is None:
        one_mode()
    else:
        pl.when(m < count)(one_mode)

        @pl.when(m == count)
        def _():
            put_tiles(row, kept, power[...])
            put_tiles(row, sent, power[...])


def inverse(row, counts, spec, ratio, q, probe, power, tabs, first, count):
    planes = count if power is None else count + 1
    last = first + count - 1
    mode = lambda m: jnp.minimum(m + first, last)
    if power is None:
        body = lambda *refs: inverse_kernel(count, *refs[:6], None, *refs[6:])
    else:
        body = lambda *refs: inverse_kernel(count, *refs)
    return pl.pallas_call(
        body,
        grid=(planes,),
        in_specs=[
            smem(),
            smem(),
            pl.BlockSpec((2, 1, 2, FRAME, FRAME), lambda m: (0, mode(m), 0, 0, 0)),
            full(2, FRAME, FRAME),
            full(2, 2, FRAME, FRAME),
            pl.BlockSpec((2, 1, FRAME, FRAME), lambda m: (0, mode(m), 0, 0)),
        ]
        + ([] if power is None else [full(FRAME, FRAME)])
        + [full(FRAME, FRAME)] * 4,
        out_specs=[
            pl.BlockSpec((2, 4, 8, 1, 8, HALF), lambda m: (0, 0, 0, m, 0, 0)),
            pl.BlockSpec((2, 4, 8, 1, 8, HALF), lambda m: (0, 0, 0, m, 0, 0)),
            full(2, 2, FRAME, FRAME),
        ],
        out_shape=[shape_of(2, 4, 8, planes, 8, HALF)] * 2 + [shape_of(2, 2, FRAME, FRAME)],
        compiler_params=PARAMS,
    )(row, counts, spec, ratio, q, probe, *([] if power is None else [power]), *tabs)


def light_kernel(offsets, left, up, corner, probe, light):
    power = jnp.zeros((FRAME, FRAME), F32)
    for m in range(MODES):
        power = power + (probe[0, m] * probe[0, m] + probe[1, m] * probe[1, m])
    rows, cols = grids()
    total = jnp.zeros((FRAME, FRAME), F32)
    for source, low_row, low_col in ((offsets, 0, 0), (left, 0, 1), (up, 1, 0), (corner, 1, 1)):
        for s in range(2):
            r, c = spot(source, s)
            keep = ((rows < r) if low_row else (rows >= r)) & ((cols < c) if low_col else (cols >= c))
            moved = source[2, s].astype(F32) * rolled(power, r, c)
            total = total + jnp.where(keep, moved, 0.0)
    light[...] = total


def light_of(offsets, left, up, corner, probe):
    return pl.pallas_call(
        light_kernel,
        in_specs=[smem()] * 4 + [vmem()],
        out_specs=vmem(),
        out_shape=shape_of(FRAME, FRAME),
        compiler_params=PARAMS,
    )(offsets, left, up, corner, probe)


def place_kernel(offsets, n0, n1, n2, mod, low, side, own):
    rows, cols = grids()
    pieces = []
    for s in range(2):
        r, c = spot(offsets, s)
        a, b = (n0[s, i] + n1[s, i] + n2[s, i] for i in range(2))
        real = rolled(a * mod[0] + b * mod[1], r, c)
        imag = rolled(b * mod[0] - a * mod[1], r, c)
        pieces.append((rows < r, cols < c, (real, imag)))
    for tile, out in ((2, low.at[0]), (3, low.at[1]), (1, side), (0, own)):
        for i in range(2):
            total = jnp.zeros((FRAME, FRAME), F32)
            for low_row, low_col, values in pieces:
                keep = (low_row if tile // 2 else ~low_row) & (low_col if tile % 2 else ~low_col)
                total = total + jnp.where(keep, values[i], 0.0)
            out[i] = total


def place(offsets, numers, mod):
    return pl.pallas_call(
        place_kernel,
        in_specs=[smem()] + [vmem()] * 4,
        out_specs=[vmem()] * 3,
        out_shape=[shape_of(2, 2, FRAME, FRAME)] + [shape_of(2, FRAME, FRAME)] * 2,
        compiler_params=PARAMS,
    )(offsets, *numers, mod)


def update_kernel(index, field, own, above, left, light, out, row_1, row_2, col_1, col_2):
    odd_row, odd_col = index[0] % 2 == 1, index[1] % 2 == 1
    inverse_light = 1.0 / (light[...] + OBJECT_DELTA)
    for i in range(2):
        value = field[i] + (own[i] + above[0, i] + left[i]) * inverse_light
        out[i] = value
        top, bottom = value[0], value[FRAME - 1]
        first, last = value[:, :HALF].T[0], value[:, HALF:].T[HALF - 1]
        row_1[i] = jnp.where(odd_row, top, bottom)
        row_2[i] = jnp.where(odd_row, bottom, top)
        col_1[i] = jnp.where(odd_col, first, last)
        col_2[i] = jnp.where(odd_col, last, first)


def update(index, field, own, above, left, light):
    return pl.pallas_call(
        update_kernel,
        in_specs=[smem()] + [vmem()] * 5,
        out_specs=[vmem()] * 5,
        out_shape=[shape_of(2, FRAME, FRAME)] + [shape_of(2, FRAME)] * 4,
        compiler_params=PARAMS,
    )(index, field, own, above, left, light)


def smooth_kernel(index, field, row_1, row_2, col_1, col_2, out):
    odd_row, odd_col = index[0] % 2 == 1, index[1] % 2 == 1
    rows, cols = grids()
    for i in range(2):
        value = field[i]
        above = jnp.where(odd_row, row_1[i], row_2[i])[None, :]
        below = jnp.where(odd_row, row_2[i], row_1[i])[None, :]
        column = lambda edge: jnp.broadcast_to(edge[None, :], (HALF, FRAME)).T
        wide = lambda edge: jnp.concatenate([column(edge), column(edge)], axis=1)
        left = wide(jnp.where(odd_col, col_1[i], col_2[i]))
        right = wide(jnp.where(odd_col, col_2[i], col_1[i]))
        north = jnp.where(rows == 0, above, pltpu.roll(value, 1, axis=0))
        south = jnp.where(rows == FRAME - 1, below, pltpu.roll(value, FRAME - 1, axis=0))
        west = jnp.where(cols == 0, left, pltpu.roll(value, 1, axis=1))
        east = jnp.where(cols == FRAME - 1, right, pltpu.roll(value, FRAME - 1, axis=1))
        out[i] = value + SMOOTH_WEIGHT * (north + south + east + west - 4.0 * value)


def smooth(index, field, *edges):
    return pl.pallas_call(
        smooth_kernel,
        in_specs=[smem()] + [vmem()] * 5,
        out_specs=vmem(),
        out_shape=shape_of(2, FRAME, FRAME),
        compiler_params=PARAMS,
    )(index, field, *edges)


ORDER = ((0, 3, 1, 2), (0, 1, 3, 2))


def gather_kernel(half, index, *refs):
    out, buffer, sem = refs[-3:]
    copies = []
    for other in range(2):
        target = (index[0] + other) % 2
        for part in range(2):
            piece = refs[2 * other + part]
            for k in range(2):
                for m in range(MODES):
                    for place in range(8):
                        i, j = place // 2, place % 2
                        buffer[
                            other, part, k, m, 8 * i : 8 * i + 8, HALF * j : HALF * j + HALF
                        ] = piece[k, place, m]
                quarter = ORDER[part][2 * half + k] ^ (index[0] // 2)
                rows = pl.ds(pl.multiple_of(64 * quarter + 32 * part, 32), 32)
                copy = pltpu.make_async_copy(
                    buffer.at[other, part, k], out.at[target, :, rows], sem.at[other, part, k]
                )
                copy.start()
                copies.append(copy)
    for copy in copies:
        copy.wait()


def gather(index, pieces, half, target=None):
    anywhere = pl.BlockSpec(memory_space=pl.ANY)
    return pl.pallas_call(
        lambda *refs: gather_kernel(half, *refs),
        in_specs=[smem()] + [vmem()] * 4 + ([] if target is None else [anywhere]),
        out_specs=anywhere,
        out_shape=shape_of(2, MODES, FRAME, FRAME),
        scratch_shapes=[
            pltpu.VMEM((2, 2, 2, MODES, 32, FRAME), F32),
            pltpu.SemaphoreType.DMA((2, 2, 2)),
        ],
        input_output_aliases={} if target is None else {5: 0},
        compiler_params=PARAMS,
    )(index, *pieces, *([] if target is None else [target]))


def shifted(value, axis, steps):
    count = lax.axis_size(axis)
    first, last = (max(0, -steps), min(count, count - steps))
    return lax.ppermute(value, axis, [(source, source + steps) for source in range(first, last)])


def flip_patterns(patterns):
    rows = jnp.concatenate([patterns[:, :HALF], jnp.flip(patterns[:, HALF:], 1)], axis=1)
    return jnp.concatenate([rows[:, :, :HALF], jnp.flip(rows[:, :, HALF:], 2)], axis=2)


def swap_y(value, bits):
    return lax.ppermute(value, "row", [(r, r ^ (2 * bits)) for r in range(8)])


def swap_core(value):
    return lax.ppermute(value, "row", [(r, r ^ 1) for r in range(8)])


def per_device(object_field, probe_modes, patterns, offsets, counts):
    tabs, mod = tables()
    row_index, col = lax.axis_index("row"), lax.axis_index("col")
    y, core = row_index // 2, row_index % 2
    row = jnp.where(lax.iota(jnp.int32, 2) == 0, row_index, col)
    live = (lax.broadcasted_iota(jnp.int32, (3, 2), 1) < counts[0]).astype(jnp.int32)
    kind = lax.broadcasted_iota(jnp.int32, (3, 2), 0)
    slots = jnp.where(kind == 2, live, jnp.pad(offsets, ((0, 1), (0, 0))))

    right_a = shifted(object_field[:, :HALF], "col", -1)
    right_b = shifted(object_field[:, HALF:], "col", -1)
    below = shifted(object_field, "row", -1)
    diag_a = shifted(right_a, "row", -1)
    diag_b = shifted(right_b, "row", -1)
    from_left = shifted(slots, "col", 1)
    from_up = shifted(slots, "row", 1)
    corner_pairs = [(r * 16 + c, r * 16 + c + 17) for r in range(7) for c in range(15)]
    from_corner = lax.ppermute(slots, ("row", "col"), corner_pairs)
    patt = flip_patterns(patterns)

    tiles = (object_field, right_a, right_b, below, diag_a, diag_b)
    spec, ratio, q, power = forward(offsets, counts, tiles, mod, probe_modes, patt, tabs)
    common = (row, counts, spec, ratio, q, probe_modes)
    kept_a, sent_a, numer_a = inverse(*common, power, tabs, 0, 4)
    other_a = swap_core(sent_a)
    kept_b, sent_b, numer_b = inverse(*common, None, tabs, 4, 2)
    other_b = swap_core(sent_b)
    total_a = jnp.add(kept_a, other_a)
    y1_a = [swap_y(total_a[0, 2:], 1), swap_y(total_a[1, 2:], 3)]
    kept_c, sent_c, numer_c = inverse(*common, None, tabs, 6, 2)
    other_c = swap_core(sent_c)
    low, side, own = place(offsets, (numer_a, numer_b, numer_c), mod)
    total_c = jnp.concatenate([kept_b + other_b, kept_c + other_c], axis=3)
    y1_c = [swap_y(total_c[0, 2:], 1), swap_y(total_c[1, 2:], 3)]
    done_a = [jnp.add(total_a[i, :2], y1_a[i]) for i in range(2)]
    y2_a = [swap_y(done_a[0][1], 3), swap_y(done_a[1][1], 1)]
    done_c = [jnp.add(total_c[i, :2], y1_c[i]) for i in range(2)]
    y2_c = [swap_y(done_c[0][1], 3), swap_y(done_c[1][1], 1)]
    above = shifted(low, "row", 1)
    mine = jnp.concatenate(
        [
            jnp.concatenate([done_a[i][0] + y2_a[i], done_c[i][0] + y2_c[i]], axis=1)
            for i in range(2)
        ],
        axis=0,
    )
    exchange = lambda value: lax.all_to_all(value, "col", split_axis=0, concat_axis=0, tiled=True)
    parts = exchange(mine)
    sums = jnp.sum(parts, axis=0)
    gradient = jnp.concatenate([sums[:4], sums[5:]], axis=0)
    tile = y * 16 + col
    old = lax.dynamic_slice(
        probe_modes, (core, 0, tile // 2 * 8, tile % 2 * HALF), (1, MODES, 8, HALF)
    )[0]
    fresh = old + gradient / (sums[4] + PROBE_DELTA)
    spread = jnp.broadcast_to(fresh[None], (16,) + fresh.shape)
    from_side = shifted(side + above[1], "col", 1)
    piece = exchange(spread)
    a, b = piece[:8], piece[8:]
    pair_a = jnp.stack([a, swap_y(a, 3)])
    pair_b = jnp.stack([b, swap_y(b, 1)])
    last_a = swap_y(pair_a, 1)
    last_b = swap_y(pair_b, 3)
    far_a, far_b = swap_core(pair_a), swap_core(pair_b)
    end_a, end_b = swap_core(last_a), swap_core(last_b)
    half_probe = gather(row, (pair_a, pair_b, far_a, far_b), 0)
    new_probe = gather(row, (last_a, last_b, end_a, end_b), 1, half_probe)

    light = light_of(slots, from_left, from_up, from_corner, probe_modes)
    updated, *edges = update(row, object_field, own, above, from_side, light)
    between = lambda count: [(i, i ^ 1) for i in range(count)]
    across = lambda count: [(i, ((i + 1) ^ 1) - 1) for i in range(1, count - 1)]
    arrived = [
        lax.ppermute(edges[0], "row", between(8)),
        lax.ppermute(edges[1], "row", across(8)),
        lax.ppermute(edges[2], "col", between(16)),
        lax.ppermute(edges[3], "col", across(16)),
    ]
    new_object = smooth(row, updated, *arrived)
    return (new_object, new_probe)


def solution(mesh):
    return jax.shard_map(
        per_device,
        mesh=mesh,
        in_specs=(
            P(None, "row", "col"),
            P(),
            P(("row", "col"), None, None),
            P(None, ("row", "col")),
            P(("row", "col")),
        ),
        out_specs=(P(None, "row", "col"), P()),
        check_vma=False,
    )
```

```python
import math

import jax
import jax.numpy as jnp
import numpy as np
from jax import lax
from jax.experimental import pallas as pl
from jax.experimental.pallas import tpu as pltpu
from jax.sharding import PartitionSpec as P

INTENSITY_FLOOR = 0.1
OBJECT_DELTA = 0.5
PROBE_DELTA = 1.0
SMOOTH_WEIGHT = 0.1
FRAME = 256
HALF = 128
MODES = 8
F32 = jnp.float32
BF16 = jnp.bfloat16
PARAMS = pltpu.CompilerParams(vmem_limit_bytes=58 * 1024 * 1024)


def tables():
    k = np.arange(HALF)[:, None] + 0.5
    x = np.arange(FRAME)[None, :]
    angle = 2.0 * math.pi * k * x / FRAME
    packed = np.concatenate([np.cos(angle), np.sin(angle)], axis=0) / math.sqrt(FRAME)
    high = packed.astype(np.float32).astype(jnp.bfloat16)
    low = (packed - high.astype(np.float64)).astype(np.float32).astype(jnp.bfloat16)
    ramp = np.arange(FRAME)
    phase = math.pi * (ramp[:, None] + ramp[None, :]) / FRAME
    mod = np.stack([np.cos(phase), np.sin(phase)]).astype(np.float32)
    return (high, low, high.T.copy(), low.T.copy()), mod


def full(*shape):
    return pl.BlockSpec(shape, lambda m: (0,) * len(shape))


def smem():
    return pl.BlockSpec(memory_space=pltpu.SMEM)


def vmem():
    return pl.BlockSpec(memory_space=pltpu.VMEM)


def shape_of(*shape):
    return jax.ShapeDtypeStruct(shape, F32)


def split(value):
    high = value.astype(BF16)
    return high, (value - high.astype(F32)).astype(BF16)


def mm(a, b):
    return jnp.dot(a, b, preferred_element_type=F32)


def two_sided(real, imag, left, right):
    parts = []
    for value in (real, imag):
        high, low = split(value)
        parts.append(mm(high, right[0]) + mm(low, right[0]) + mm(high, right[1]))
    results = []
    for part in parts:
        high, low = split(part)
        both = mm(left[0], high)
        results.append(both[:FRAME] + both[FRAME:] + mm(left[1], low))
    return results


def quarters(value):
    return value[:HALF, :HALF], value[:HALF, HALF:], value[HALF:, :HALF], value[HALF:, HALF:]


def grids():
    rows = lax.broadcasted_iota(jnp.int32, (FRAME, FRAME), 0)
    cols = lax.broadcasted_iota(jnp.int32, (FRAME, FRAME), 1)
    return rows, cols


def rolled(value, r, c):
    return pltpu.roll(pltpu.roll(value, r, axis=0), c, axis=1)


def spot(offsets, s):
    return offsets[0, s] & (FRAME - 1), offsets[1, s] & (FRAME - 1)


def alive(counts, s):
    return (s < counts[0]).astype(F32)


def forward_kernel(
    offsets, counts, own, right, below, diag, mod, probe, patt, ph, plo, pth, ptl, spec, ratio, q, power, inten
):
    m = pl.program_id(0)

    @pl.when(m == 0)
    def _():
        rows, cols = grids()
        total = jnp.zeros((FRAME, FRAME), F32)
        for s in range(2):
            r, c = spot(offsets, s)
            parts = []
            for i in range(2):
                top = jnp.where(cols < c, right[i], own[i])
                bottom = jnp.where(cols < c, diag[i], below[i])
                tile = jnp.where(rows < r, bottom, top)
                parts.append(rolled(tile, lax.rem(FRAME - r, FRAME), lax.rem(FRAME - c, FRAME)))
            a, b = parts
            total = total + alive(counts, s) * (a * a + b * b)
            q[s, 0] = a * mod[0] - b * mod[1]
            q[s, 1] = a * mod[1] + b * mod[0]
            inten[s] = jnp.zeros((FRAME, FRAME), F32)
        power[...] = total

    pr, pi = probe[0, 0], probe[1, 0]
    for s in range(2):
        qr, qi = q[s, 0], q[s, 1]
        wr, wi = pr * qr - pi * qi, pr * qi + pi * qr
        mr, mi = two_sided(wr, wi, (jnp.concatenate([ph[...], plo[...]], axis=0), ph[...]), (pth[...], ptl[...]))
        acc, acs, asc, ass = quarters(mr)
        bcc, bcs, bsc, bss = quarters(mi)
        e1, e2 = acc - ass, acc + ass
        f1, f2 = bcs + bsc, bsc - bcs
        g1, g2 = bcc - bss, bcc + bss
        h1, h2 = acs + asc, acs - asc
        quads = (
            (0, 0, e1 + f1, g1 - h1),
            (0, HALF, e2 + f2, g2 + h2),
            (HALF, 0, e2 - f2, g2 - h2),
            (HALF, HALF, e1 - f1, g1 + h1),
        )
        for y, x, re, im in quads:
            spec[s, 0, 0, pl.ds(y, HALF), pl.ds(x, HALF)] = re
            spec[s, 0, 1, pl.ds(y, HALF), pl.ds(x, HALF)] = im
            inten[s, pl.ds(y, HALF), pl.ds(x, HALF)] += re * re + im * im

    @pl.when(m == MODES - 1)
    def _():
        for s in range(2):
            ratio[s] = patt[s] / jnp.sqrt(jnp.maximum(inten[s], INTENSITY_FLOOR))


def forward(offsets, counts, tiles, mod, probe, patt, tabs):
    return pl.pallas_call(
        forward_kernel,
        grid=(MODES,),
        in_specs=[smem()] * 2
        + [full(2, FRAME, FRAME)] * 5
        + [pl.BlockSpec((2, 1, FRAME, FRAME), lambda m: (0, m, 0, 0)), full(2, FRAME, FRAME)]
        + [full(FRAME, FRAME)] * 4,
        out_specs=[
            pl.BlockSpec((2, 1, 2, FRAME, FRAME), lambda m: (0, m, 0, 0, 0)),
            full(2, FRAME, FRAME),
            full(2, 2, FRAME, FRAME),
            full(FRAME, FRAME),
        ],
        out_shape=[
            shape_of(2, MODES, 2, FRAME, FRAME),
            shape_of(2, FRAME, FRAME),
            shape_of(2, 2, FRAME, FRAME),
            shape_of(FRAME, FRAME),
        ],
        scratch_shapes=[pltpu.VMEM((2, FRAME, FRAME), F32)],
        compiler_params=PARAMS,
    )(offsets, counts, *tiles, mod, probe, patt, *tabs)


def quarter_place(row, part, t):
    v = (t // 16) ^ (row[0] // 2)
    if part == 1:
        return v ^ (v >> 1)
    return jnp.where(v == 0, 0, jnp.where(v == 3, 1, v + 1))


def put_tiles(row, ref, value):
    for t in range(64):
        part, place = t % 16 // 8, t % 8
        where = quarter_place(row, part, t)
        i, j = t // 2, t % 2
        ref[part, where, place, 0] = value[8 * i : 8 * i + 8, HALF * j : HALF * j + HALF]


def inverse_kernel(count, row, counts, spec, ratio, q, probe, power, ph, plo, pth, ptl, kept, sent, numer):
    m = pl.program_id(0)

    @pl.when(m == 0)
    def _():
        numer[...] = jnp.zeros_like(numer)

    def one_mode():
        pr, pi = probe[0, 0], probe[1, 0]
        gr = jnp.zeros((FRAME, FRAME), F32)
        gi = jnp.zeros((FRAME, FRAME), F32)
        for s in range(2):
            live = alive(counts, s)
            rq = quarters(ratio[s])
            re = [a * b for a, b in zip(quarters(spec[s, 0, 0]), rq)]
            im = [a * b for a, b in zip(quarters(spec[s, 0, 1]), rq)]
            s1r, d1r, s2r, d2r = re[0] + re[3], re[0] - re[3], re[1] + re[2], re[1] - re[2]
            s1i, d1i, s2i, d2i = im[0] + im[3], im[3] - im[0], im[1] + im[2], im[1] - im[2]
            join = lambda a, b, axis: jnp.concatenate([a, b], axis=axis)
            ur = join(join(s1r + s2r, d1i + d2i, 1), join(d1i - d2i, s2r - s1r, 1), 0)
            ui = join(join(s1i + s2i, d1r - d2r, 1), join(d1r + d2r, s2i - s1i, 1), 0)
            nr, ni = two_sided(ur, ui, (jnp.concatenate([pth[...], ptl[...]], axis=0), pth[...]), (ph[...], plo[...]))
            qr, qi = q[s, 0], q[s, 1]
            dr = (nr - (pr * qr - pi * qi)) * live
            di = (ni - (pr * qi + pi * qr)) * live
            numer[s, 0] += pr * dr + pi * di
            numer[s, 1] += pr * di - pi * dr
            gr = gr + (qr * dr + qi * di)
            gi = gi + (qr * di - qi * dr)
        first_core = row[0] % 2 == 0
        put_tiles(row, kept, jnp.where(first_core, gr, gi))
        put_tiles(row, sent, jnp.where(first_core, gi, gr))

    if power is None:
        one_mode()
    else:
        pl.when(m < count)(one_mode)

        @pl.when(m == count)
        def _():
            put_tiles(row, kept, power[...])
            put_tiles(row, sent, power[...])


def inverse(row, counts, spec, ratio, q, probe, power, tabs, first, count):
    planes = count if power is None else count + 1
    last = first + count - 1
    mode = lambda m: jnp.minimum(m + first, last)
    if power is None:
        body = lambda *refs: inverse_kernel(count, *refs[:6], None, *refs[6:])
    else:
        body = lambda *refs: inverse_kernel(count, *refs)
    return pl.pallas_call(
        body,
        grid=(planes,),
        in_specs=[
            smem(),
            smem(),
            pl.BlockSpec((2, 1, 2, FRAME, FRAME), lambda m: (0, mode(m), 0, 0, 0)),
            full(2, FRAME, FRAME),
            full(2, 2, FRAME, FRAME),
            pl.BlockSpec((2, 1, FRAME, FRAME), lambda m: (0, mode(m), 0, 0)),
        ]
        + ([] if power is None else [full(FRAME, FRAME)])
        + [full(FRAME, FRAME)] * 4,
        out_specs=[
            pl.BlockSpec((2, 4, 8, 1, 8, HALF), lambda m: (0, 0, 0, m, 0, 0)),
            pl.BlockSpec((2, 4, 8, 1, 8, HALF), lambda m: (0, 0, 0, m, 0, 0)),
            full(2, 2, FRAME, FRAME),
        ],
        out_shape=[shape_of(2, 4, 8, planes, 8, HALF)] * 2 + [shape_of(2, 2, FRAME, FRAME)],
        compiler_params=PARAMS,
    )(row, counts, spec, ratio, q, probe, *([] if power is None else [power]), *tabs)


def light_kernel(offsets, left, up, corner, probe, light):
    power = jnp.zeros((FRAME, FRAME), F32)
    for m in range(MODES):
        power = power + (probe[0, m] * probe[0, m] + probe[1, m] * probe[1, m])
    rows, cols = grids()
    total = jnp.zeros((FRAME, FRAME), F32)
    for source, low_row, low_col in ((offsets, 0, 0), (left, 0, 1), (up, 1, 0), (corner, 1, 1)):
        for s in range(2):
            r, c = spot(source, s)
            keep = ((rows < r) if low_row else (rows >= r)) & ((cols < c) if low_col else (cols >= c))
            moved = source[2, s].astype(F32) * rolled(power, r, c)
            total = total + jnp.where(keep, moved, 0.0)
    light[...] = total


def light_of(offsets, left, up, corner, probe):
    return pl.pallas_call(
        light_kernel,
        in_specs=[smem()] * 4 + [vmem()],
        out_specs=vmem(),
        out_shape=shape_of(FRAME, FRAME),
        compiler_params=PARAMS,
    )(offsets, left, up, corner, probe)


def place_kernel(offsets, n0, n1, n2, mod, low, side, own):
    rows, cols = grids()
    pieces = []
    for s in range(2):
        r, c = spot(offsets, s)
        a, b = (n0[s, i] + n1[s, i] + n2[s, i] for i in range(2))
        real = rolled(a * mod[0] + b * mod[1], r, c)
        imag = rolled(b * mod[0] - a * mod[1], r, c)
        pieces.append((rows < r, cols < c, (real, imag)))
    for tile, out in ((2, low.at[0]), (3, low.at[1]), (1, side), (0, own)):
        for i in range(2):
            total = jnp.zeros((FRAME, FRAME), F32)
            for low_row, low_col, values in pieces:
                keep = (low_row if tile // 2 else ~low_row) & (low_col if tile % 2 else ~low_col)
                total = total + jnp.where(keep, values[i], 0.0)
            out[i] = total


def place(offsets, numers, mod):
    return pl.pallas_call(
        place_kernel,
        in_specs=[smem()] + [vmem()] * 4,
        out_specs=[vmem()] * 3,
        out_shape=[shape_of(2, 2, FRAME, FRAME)] + [shape_of(2, FRAME, FRAME)] * 2,
        compiler_params=PARAMS,
    )(offsets, *numers, mod)


def update_kernel(index, field, own, above, left, light, out, row_1, row_2, col_1, col_2):
    odd_row, odd_col = index[0] % 2 == 1, index[1] % 2 == 1
    inverse_light = 1.0 / (light[...] + OBJECT_DELTA)
    for i in range(2):
        value = field[i] + (own[i] + above[0, i] + left[i]) * inverse_light
        out[i] = value
        top, bottom = value[0], value[FRAME - 1]
        first, last = value[:, :HALF].T[0], value[:, HALF:].T[HALF - 1]
        row_1[i] = jnp.where(odd_row, top, bottom)
        row_2[i] = jnp.where(odd_row, bottom, top)
        col_1[i] = jnp.where(odd_col, first, last)
        col_2[i] = jnp.where(odd_col, last, first)


def update(index, field, own, above, left, light):
    return pl.pallas_call(
        update_kernel,
        in_specs=[smem()] + [vmem()] * 5,
        out_specs=[vmem()] * 5,
        out_shape=[shape_of(2, FRAME, FRAME)] + [shape_of(2, FRAME)] * 4,
        compiler_params=PARAMS,
    )(index, field, own, above, left, light)


def smooth_kernel(index, field, row_1, row_2, col_1, col_2, out):
    odd_row, odd_col = index[0] % 2 == 1, index[1] % 2 == 1
    rows, cols = grids()
    for i in range(2):
        value = field[i]
        above = jnp.where(odd_row, row_1[i], row_2[i])[None, :]
        below = jnp.where(odd_row, row_2[i], row_1[i])[None, :]
        column = lambda edge: jnp.broadcast_to(edge[None, :], (HALF, FRAME)).T
        wide = lambda edge: jnp.concatenate([column(edge), column(edge)], axis=1)
        left = wide(jnp.where(odd_col, col_1[i], col_2[i]))
        right = wide(jnp.where(odd_col, col_2[i], col_1[i]))
        north = jnp.where(rows == 0, above, pltpu.roll(value, 1, axis=0))
        south = jnp.where(rows == FRAME - 1, below, pltpu.roll(value, FRAME - 1, axis=0))
        west = jnp.where(cols == 0, left, pltpu.roll(value, 1, axis=1))
        east = jnp.where(cols == FRAME - 1, right, pltpu.roll(value, FRAME - 1, axis=1))
        out[i] = value + SMOOTH_WEIGHT * (north + south + east + west - 4.0 * value)


def smooth(index, field, *edges):
    return pl.pallas_call(
        smooth_kernel,
        in_specs=[smem()] + [vmem()] * 5,
        out_specs=vmem(),
        out_shape=shape_of(2, FRAME, FRAME),
        compiler_params=PARAMS,
    )(index, field, *edges)


ORDER = ((0, 3, 1, 2), (0, 1, 3, 2))


def gather_kernel(half, index, *refs):
    out, buffer, sem = refs[-3:]
    copies = []
    for other in range(2):
        target = (index[0] + other) % 2
        for part in range(2):
            piece = refs[2 * other + part]
            for k in range(2):
                for m in range(MODES):
                    for place in range(8):
                        i, j = place // 2, place % 2
                        buffer[
                            other, part, k, m, 8 * i : 8 * i + 8, HALF * j : HALF * j + HALF
                        ] = piece[k, place, m]
                quarter = ORDER[part][2 * half + k] ^ (index[0] // 2)
                rows = pl.ds(pl.multiple_of(64 * quarter + 32 * part, 32), 32)
                copy = pltpu.make_async_copy(
                    buffer.at[other, part, k], out.at[target, :, rows], sem.at[other, part, k]
                )
                copy.start()
                copies.append(copy)
    for copy in copies:
        copy.wait()


def gather(index, pieces, half, target=None):
    anywhere = pl.BlockSpec(memory_space=pl.ANY)
    return pl.pallas_call(
        lambda *refs: gather_kernel(half, *refs),
        in_specs=[smem()] + [vmem()] * 4 + ([] if target is None else [anywhere]),
        out_specs=anywhere,
        out_shape=shape_of(2, MODES, FRAME, FRAME),
        scratch_shapes=[
            pltpu.VMEM((2, 2, 2, MODES, 32, FRAME), F32),
            pltpu.SemaphoreType.DMA((2, 2, 2)),
        ],
        input_output_aliases={} if target is None else {5: 0},
        compiler_params=PARAMS,
    )(index, *pieces, *([] if target is None else [target]))


def shifted(value, axis, steps):
    count = lax.axis_size(axis)
    first, last = (max(0, -steps), min(count, count - steps))
    return lax.ppermute(value, axis, [(source, source + steps) for source in range(first, last)])


def flip_patterns(patterns):
    rows = jnp.concatenate([patterns[:, :HALF], jnp.flip(patterns[:, HALF:], 1)], axis=1)
    return jnp.concatenate([rows[:, :, :HALF], jnp.flip(rows[:, :, HALF:], 2)], axis=2)


def swap_y(value, bits):
    return lax.ppermute(value, "row", [(r, r ^ (2 * bits)) for r in range(8)])


def swap_core(value):
    return lax.ppermute(value, "row", [(r, r ^ 1) for r in range(8)])


def per_device(object_field, probe_modes, patterns, offsets, counts):
    tabs, mod = tables()
    row_index, col = lax.axis_index("row"), lax.axis_index("col")
    y, core = row_index // 2, row_index % 2
    row = jnp.where(lax.iota(jnp.int32, 2) == 0, row_index, col)
    live = (lax.broadcasted_iota(jnp.int32, (3, 2), 1) < counts[0]).astype(jnp.int32)
    kind = lax.broadcasted_iota(jnp.int32, (3, 2), 0)
    slots = jnp.where(kind == 2, live, jnp.pad(offsets, ((0, 1), (0, 0))))

    right = shifted(object_field, "col", -1)
    below = shifted(object_field, "row", -1)
    diag = shifted(right, "row", -1)
    from_left = shifted(slots, "col", 1)
    from_up = shifted(slots, "row", 1)
    corner_pairs = [(r * 16 + c, r * 16 + c + 17) for r in range(7) for c in range(15)]
    from_corner = lax.ppermute(slots, ("row", "col"), corner_pairs)
    patt = flip_patterns(patterns)

    tiles = (object_field, right, below, diag)
    spec, ratio, q, power = forward(offsets, counts, tiles, mod, probe_modes, patt, tabs)
    common = (row, counts, spec, ratio, q, probe_modes)
    kept_a, sent_a, numer_a = inverse(*common, power, tabs, 0, 4)
    other_a = swap_core(sent_a)
    kept_b, sent_b, numer_b = inverse(*common, None, tabs, 4, 2)
    other_b = swap_core(sent_b)
    total_a = jnp.add(kept_a, other_a)
    y1_a = [swap_y(total_a[0, 2:], 1), swap_y(total_a[1, 2:], 3)]
    kept_c, sent_c, numer_c = inverse(*common, None, tabs, 6, 2)
    other_c = swap_core(sent_c)
    low, side, own = place(offsets, (numer_a, numer_b, numer_c), mod)
    total_c = jnp.concatenate([kept_b + other_b, kept_c + other_c], axis=3)
    y1_c = [swap_y(total_c[0, 2:], 1), swap_y(total_c[1, 2:], 3)]
    done_a = [jnp.add(total_a[i, :2], y1_a[i]) for i in range(2)]
    y2_a = [swap_y(done_a[0][1], 3), swap_y(done_a[1][1], 1)]
    done_c = [jnp.add(total_c[i, :2], y1_c[i]) for i in range(2)]
    y2_c = [swap_y(done_c[0][1], 3), swap_y(done_c[1][1], 1)]
    above = shifted(low, "row", 1)
    mine = jnp.concatenate(
        [
            jnp.concatenate([done_a[i][0] + y2_a[i], done_c[i][0] + y2_c[i]], axis=1)
            for i in range(2)
        ],
        axis=0,
    )
    exchange = lambda value: lax.all_to_all(value, "col", split_axis=0, concat_axis=0, tiled=True)
    parts = exchange(mine)
    sums = jnp.sum(parts, axis=0)
    gradient = jnp.concatenate([sums[:4], sums[5:]], axis=0)
    tile = y * 16 + col
    old = lax.dynamic_slice(
        probe_modes, (core, 0, tile // 2 * 8, tile % 2 * HALF), (1, MODES, 8, HALF)
    )[0]
    fresh = old + gradient / (sums[4] + PROBE_DELTA)
    spread = jnp.broadcast_to(fresh[None], (16,) + fresh.shape)
    from_side = shifted(side + above[1], "col", 1)
    piece = exchange(spread)
    a, b = piece[:8], piece[8:]
    pair_a = jnp.stack([a, swap_y(a, 3)])
    pair_b = jnp.stack([b, swap_y(b, 1)])
    last_a = swap_y(pair_a, 1)
    last_b = swap_y(pair_b, 3)
    far_a, far_b = swap_core(pair_a), swap_core(pair_b)
    end_a, end_b = swap_core(last_a), swap_core(last_b)
    half_probe = gather(row, (pair_a, pair_b, far_a, far_b), 0)
    new_probe = gather(row, (last_a, last_b, end_a, end_b), 1, half_probe)

    light = light_of(slots, from_left, from_up, from_corner, probe_modes)
    updated, *edges = update(row, object_field, own, above, from_side, light)
    between = lambda count: [(i, i ^ 1) for i in range(count)]
    across = lambda count: [(i, ((i + 1) ^ 1) - 1) for i in range(1, count - 1)]
    arrived = [
        lax.ppermute(edges[0], "row", between(8)),
        lax.ppermute(edges[1], "row", across(8)),
        lax.ppermute(edges[2], "col", between(16)),
        lax.ppermute(edges[3], "col", across(16)),
    ]
    new_object = smooth(row, updated, *arrived)
    return (new_object, new_probe)


def solution(mesh):
    return jax.shard_map(
        per_device,
        mesh=mesh,
        in_specs=(
            P(None, "row", "col"),
            P(),
            P(("row", "col"), None, None),
            P(None, ("row", "col")),
            P(("row", "col")),
        ),
        out_specs=(P(None, "row", "col"), P()),
        check_vma=False,
    )
```

```python
import math

import jax
import jax.numpy as jnp
import numpy as np
from jax import lax
from jax.experimental import pallas as pl
from jax.experimental.pallas import tpu as pltpu
from jax.sharding import PartitionSpec as P

INTENSITY_FLOOR = 0.1
OBJECT_DELTA = 0.5
PROBE_DELTA = 1.0
SMOOTH_WEIGHT = 0.1
FRAME = 256
HALF = 128
MODES = 8
F32 = jnp.float32
BF16 = jnp.bfloat16
PARAMS = pltpu.CompilerParams(vmem_limit_bytes=58 * 1024 * 1024)


def tables():
    k = np.arange(HALF)[:, None] + 0.5
    x = np.arange(FRAME)[None, :]
    angle = 2.0 * math.pi * k * x / FRAME
    packed = np.concatenate([np.cos(angle), np.sin(angle)], axis=0) / math.sqrt(FRAME)
    high = packed.astype(np.float32).astype(jnp.bfloat16)
    low = (packed - high.astype(np.float64)).astype(np.float32).astype(jnp.bfloat16)
    ramp = np.arange(FRAME)
    phase = math.pi * (ramp[:, None] + ramp[None, :]) / FRAME
    mod = np.stack([np.cos(phase), np.sin(phase)]).astype(np.float32)
    return (high, low, high.T.copy(), low.T.copy()), mod


def full(*shape):
    return pl.BlockSpec(shape, lambda m: (0,) * len(shape))


def smem():
    return pl.BlockSpec(memory_space=pltpu.SMEM)


def vmem():
    return pl.BlockSpec(memory_space=pltpu.VMEM)


def shape_of(*shape):
    return jax.ShapeDtypeStruct(shape, F32)


def split(value):
    high = value.astype(BF16)
    return high, (value - high.astype(F32)).astype(BF16)


def mm(a, b):
    return jnp.dot(a, b, preferred_element_type=F32)


def two_sided(real, imag, left, right):
    parts = []
    for value in (real, imag):
        high, low = split(value)
        parts.append(mm(high, right[0]) + mm(low, right[0]) + mm(high, right[1]))
    results = []
    for part in parts:
        high, low = split(part)
        both = mm(left[0], high)
        results.append(both[:FRAME] + both[FRAME:] + mm(left[1], low))
    return results


def quarters(value):
    return value[:HALF, :HALF], value[:HALF, HALF:], value[HALF:, :HALF], value[HALF:, HALF:]


def grids():
    rows = lax.broadcasted_iota(jnp.int32, (FRAME, FRAME), 0)
    cols = lax.broadcasted_iota(jnp.int32, (FRAME, FRAME), 1)
    return rows, cols


def rolled(value, r, c):
    return pltpu.roll(pltpu.roll(value, r, axis=0), c, axis=1)


def spot(offsets, s):
    return offsets[0, s] & (FRAME - 1), offsets[1, s] & (FRAME - 1)


def alive(counts, s):
    return (s < counts[0]).astype(F32)


def forward_kernel(
    offsets, counts, own, right, below, diag, mod, probe, patt, ph, plo, pth, ptl, spec, ratio, q, power, inten
):
    m = pl.program_id(0)

    @pl.when(m == 0)
    def _():
        rows, cols = grids()
        total = jnp.zeros((FRAME, FRAME), F32)
        for s in range(2):
            r, c = spot(offsets, s)
            parts = []
            for i in range(2):
                top = jnp.where(cols < c, right[i], own[i])
                bottom = jnp.where(cols < c, diag[i], below[i])
                tile = jnp.where(rows < r, bottom, top)
                parts.append(rolled(tile, lax.rem(FRAME - r, FRAME), lax.rem(FRAME - c, FRAME)))
            a, b = parts
            total = total + alive(counts, s) * (a * a + b * b)
            q[s, 0] = a * mod[0] - b * mod[1]
            q[s, 1] = a * mod[1] + b * mod[0]
            inten[s] = jnp.zeros((FRAME, FRAME), F32)
        power[...] = total

    pr, pi = probe[0, 0], probe[1, 0]
    for s in range(2):
        qr, qi = q[s, 0], q[s, 1]
        wr, wi = pr * qr - pi * qi, pr * qi + pi * qr
        mr, mi = two_sided(wr, wi, (jnp.concatenate([ph[...], plo[...]], axis=0), ph[...]), (pth[...], ptl[...]))
        acc, acs, asc, ass = quarters(mr)
        bcc, bcs, bsc, bss = quarters(mi)
        e1, e2 = acc - ass, acc + ass
        f1, f2 = bcs + bsc, bsc - bcs
        g1, g2 = bcc - bss, bcc + bss
        h1, h2 = acs + asc, acs - asc
        quads = (
            (0, 0, e1 + f1, g1 - h1),
            (0, HALF, e2 + f2, g2 + h2),
            (HALF, 0, e2 - f2, g2 - h2),
            (HALF, HALF, e1 - f1, g1 + h1),
        )
        for y, x, re, im in quads:
            spec[s, 0, 0, pl.ds(y, HALF), pl.ds(x, HALF)] = re
            spec[s, 0, 1, pl.ds(y, HALF), pl.ds(x, HALF)] = im
            inten[s, pl.ds(y, HALF), pl.ds(x, HALF)] += re * re + im * im

    @pl.when(m == MODES - 1)
    def _():
        for s in range(2):
            ratio[s] = patt[s] / jnp.sqrt(jnp.maximum(inten[s], INTENSITY_FLOOR))


def forward(offsets, counts, tiles, mod, probe, patt, tabs):
    return pl.pallas_call(
        forward_kernel,
        grid=(MODES,),
        in_specs=[smem()] * 2
        + [full(2, FRAME, FRAME)] * 5
        + [pl.BlockSpec((2, 1, FRAME, FRAME), lambda m: (0, m, 0, 0)), full(2, FRAME, FRAME)]
        + [full(FRAME, FRAME)] * 4,
        out_specs=[
            pl.BlockSpec((2, 1, 2, FRAME, FRAME), lambda m: (0, m, 0, 0, 0)),
            full(2, FRAME, FRAME),
            full(2, 2, FRAME, FRAME),
            full(FRAME, FRAME),
        ],
        out_shape=[
            shape_of(2, MODES, 2, FRAME, FRAME),
            shape_of(2, FRAME, FRAME),
            shape_of(2, 2, FRAME, FRAME),
            shape_of(FRAME, FRAME),
        ],
        scratch_shapes=[pltpu.VMEM((2, FRAME, FRAME), F32)],
        compiler_params=PARAMS,
    )(offsets, counts, *tiles, mod, probe, patt, *tabs)


def quarter_place(row, part, t):
    v = (t // 16) ^ (row[0] // 2)
    if part == 1:
        return v ^ (v >> 1)
    return jnp.where(v == 0, 0, jnp.where(v == 3, 1, v + 1))


def put_tiles(row, ref, value):
    for t in range(64):
        part, place = t % 16 // 8, t % 8
        where = quarter_place(row, part, t)
        i, j = t // 2, t % 2
        ref[part, where, place, 0] = value[8 * i : 8 * i + 8, HALF * j : HALF * j + HALF]


def inverse_kernel(count, row, counts, spec, ratio, q, probe, power, ph, plo, pth, ptl, kept, sent, numer):
    m = pl.program_id(0)

    @pl.when(m == 0)
    def _():
        numer[...] = jnp.zeros_like(numer)

    def one_mode():
        pr, pi = probe[0, 0], probe[1, 0]
        gr = jnp.zeros((FRAME, FRAME), F32)
        gi = jnp.zeros((FRAME, FRAME), F32)
        for s in range(2):
            live = alive(counts, s)
            rq = quarters(ratio[s])
            re = [a * b for a, b in zip(quarters(spec[s, 0, 0]), rq)]
            im = [a * b for a, b in zip(quarters(spec[s, 0, 1]), rq)]
            s1r, d1r, s2r, d2r = re[0] + re[3], re[0] - re[3], re[1] + re[2], re[1] - re[2]
            s1i, d1i, s2i, d2i = im[0] + im[3], im[3] - im[0], im[1] + im[2], im[1] - im[2]
            join = lambda a, b, axis: jnp.concatenate([a, b], axis=axis)
            ur = join(join(s1r + s2r, d1i + d2i, 1), join(d1i - d2i, s2r - s1r, 1), 0)
            ui = join(join(s1i + s2i, d1r - d2r, 1), join(d1r + d2r, s2i - s1i, 1), 0)
            nr, ni = two_sided(ur, ui, (jnp.concatenate([pth[...], ptl[...]], axis=0), pth[...]), (ph[...], plo[...]))
            qr, qi = q[s, 0], q[s, 1]
            dr = (nr - (pr * qr - pi * qi)) * live
            di = (ni - (pr * qi + pi * qr)) * live
            numer[s, 0] += pr * dr + pi * di
            numer[s, 1] += pr * di - pi * dr
            gr = gr + (qr * dr + qi * di)
            gi = gi + (qr * di - qi * dr)
        first_core = row[0] % 2 == 0
        put_tiles(row, kept, jnp.where(first_core, gr, gi))
        put_tiles(row, sent, jnp.where(first_core, gi, gr))

    if power is None:
        one_mode()
    else:
        pl.when(m < count)(one_mode)

        @pl.when(m == count)
        def _():
            put_tiles(row, kept, power[...])
            put_tiles(row, sent, power[...])


def inverse(row, counts, spec, ratio, q, probe, power, tabs, first, count):
    planes = count if power is None else count + 1
    last = first + count - 1
    mode = lambda m: jnp.minimum(m + first, last)
    if power is None:
        body = lambda *refs: inverse_kernel(count, *refs[:6], None, *refs[6:])
    else:
        body = lambda *refs: inverse_kernel(count, *refs)
    return pl.pallas_call(
        body,
        grid=(planes,),
        in_specs=[
            smem(),
            smem(),
            pl.BlockSpec((2, 1, 2, FRAME, FRAME), lambda m: (0, mode(m), 0, 0, 0)),
            full(2, FRAME, FRAME),
            full(2, 2, FRAME, FRAME),
            pl.BlockSpec((2, 1, FRAME, FRAME), lambda m: (0, mode(m), 0, 0)),
        ]
        + ([] if power is None else [full(FRAME, FRAME)])
        + [full(FRAME, FRAME)] * 4,
        out_specs=[
            pl.BlockSpec((2, 4, 8, 1, 8, HALF), lambda m: (0, 0, 0, m, 0, 0)),
            pl.BlockSpec((2, 4, 8, 1, 8, HALF), lambda m: (0, 0, 0, m, 0, 0)),
            full(2, 2, FRAME, FRAME),
        ],
        out_shape=[shape_of(2, 4, 8, planes, 8, HALF)] * 2 + [shape_of(2, 2, FRAME, FRAME)],
        compiler_params=PARAMS,
    )(row, counts, spec, ratio, q, probe, *([] if power is None else [power]), *tabs)


def light_kernel(offsets, left, up, corner, probe, light):
    power = jnp.zeros((FRAME, FRAME), F32)
    for m in range(MODES):
        power = power + (probe[0, m] * probe[0, m] + probe[1, m] * probe[1, m])
    rows, cols = grids()
    total = jnp.zeros((FRAME, FRAME), F32)
    for source, low_row, low_col in ((offsets, 0, 0), (left, 0, 1), (up, 1, 0), (corner, 1, 1)):
        for s in range(2):
            r, c = spot(source, s)
            keep = ((rows < r) if low_row else (rows >= r)) & ((cols < c) if low_col else (cols >= c))
            moved = source[2, s].astype(F32) * rolled(power, r, c)
            total = total + jnp.where(keep, moved, 0.0)
    light[...] = total


def light_of(offsets, left, up, corner, probe):
    return pl.pallas_call(
        light_kernel,
        in_specs=[smem()] * 4 + [vmem()],
        out_specs=vmem(),
        out_shape=shape_of(FRAME, FRAME),
        compiler_params=PARAMS,
    )(offsets, left, up, corner, probe)


def place_kernel(offsets, n0, n1, n2, mod, low, side, own):
    rows, cols = grids()
    pieces = []
    for s in range(2):
        r, c = spot(offsets, s)
        a, b = (n0[s, i] + n1[s, i] + n2[s, i] for i in range(2))
        real = rolled(a * mod[0] + b * mod[1], r, c)
        imag = rolled(b * mod[0] - a * mod[1], r, c)
        pieces.append((rows < r, cols < c, (real, imag)))
    for tile, out in ((2, low.at[0]), (3, low.at[1]), (1, side), (0, own)):
        for i in range(2):
            total = jnp.zeros((FRAME, FRAME), F32)
            for low_row, low_col, values in pieces:
                keep = (low_row if tile // 2 else ~low_row) & (low_col if tile % 2 else ~low_col)
                total = total + jnp.where(keep, values[i], 0.0)
            out[i] = total


def place(offsets, numers, mod):
    return pl.pallas_call(
        place_kernel,
        in_specs=[smem()] + [vmem()] * 4,
        out_specs=[vmem()] * 3,
        out_shape=[shape_of(2, 2, FRAME, FRAME)] + [shape_of(2, FRAME, FRAME)] * 2,
        compiler_params=PARAMS,
    )(offsets, *numers, mod)


def update_kernel(index, field, own, above, left, light, out, row_1, row_2, col_1, col_2):
    odd_row, odd_col = index[0] % 2 == 1, index[1] % 2 == 1
    inverse_light = 1.0 / (light[...] + OBJECT_DELTA)
    for i in range(2):
        value = field[i] + (own[i] + above[0, i] + left[i]) * inverse_light
        out[i] = value
        top, bottom = value[0], value[FRAME - 1]
        first, last = value[:, :HALF].T[0], value[:, HALF:].T[HALF - 1]
        row_1[i] = jnp.where(odd_row, top, bottom)
        row_2[i] = jnp.where(odd_row, bottom, top)
        col_1[i] = jnp.where(odd_col, first, last)
        col_2[i] = jnp.where(odd_col, last, first)


def update(index, field, own, above, left, light):
    return pl.pallas_call(
        update_kernel,
        in_specs=[smem()] + [vmem()] * 5,
        out_specs=[vmem()] * 5,
        out_shape=[shape_of(2, FRAME, FRAME)] + [shape_of(2, FRAME)] * 4,
        compiler_params=PARAMS,
    )(index, field, own, above, left, light)


def smooth_kernel(index, field, row_1, row_2, col_1, col_2, out):
    odd_row, odd_col = index[0] % 2 == 1, index[1] % 2 == 1
    rows, cols = grids()
    for i in range(2):
        value = field[i]
        above = jnp.where(odd_row, row_1[i], row_2[i])[None, :]
        below = jnp.where(odd_row, row_2[i], row_1[i])[None, :]
        column = lambda edge: jnp.broadcast_to(edge[None, :], (HALF, FRAME)).T
        wide = lambda edge: jnp.concatenate([column(edge), column(edge)], axis=1)
        left = wide(jnp.where(odd_col, col_1[i], col_2[i]))
        right = wide(jnp.where(odd_col, col_2[i], col_1[i]))
        north = jnp.where(rows == 0, above, pltpu.roll(value, 1, axis=0))
        south = jnp.where(rows == FRAME - 1, below, pltpu.roll(value, FRAME - 1, axis=0))
        west = jnp.where(cols == 0, left, pltpu.roll(value, 1, axis=1))
        east = jnp.where(cols == FRAME - 1, right, pltpu.roll(value, FRAME - 1, axis=1))
        out[i] = value + SMOOTH_WEIGHT * (north + south + east + west - 4.0 * value)


def smooth(index, field, *edges):
    return pl.pallas_call(
        smooth_kernel,
        in_specs=[smem()] + [vmem()] * 5,
        out_specs=vmem(),
        out_shape=shape_of(2, FRAME, FRAME),
        compiler_params=PARAMS,
    )(index, field, *edges)


ORDER = ((0, 3, 1, 2), (0, 1, 3, 2))


def gather_kernel(index, *refs):
    out, loaded, buffer, load_sem, sem = refs[-5:]
    loads = [pltpu.make_async_copy(refs[i], loaded.at[i], load_sem.at[i]) for i in range(8)]
    for load in loads:
        load.start()
    copies = []
    for n in range(8):
        half, other, part = n // 4, n // 2 % 2, n % 2
        loads[n].wait()
        for k in range(2):
            for m in range(MODES):
                for place in range(8):
                    i, j = place // 2, place % 2
                    buffer[n, k, m, 8 * i : 8 * i + 8, HALF * j : HALF * j + HALF] = loaded[
                        n, k, place, m
                    ]
            quarter = ORDER[part][2 * half + k] ^ (index[0] // 2)
            rows = pl.ds(pl.multiple_of(64 * quarter + 32 * part, 32), 32)
            copy = pltpu.make_async_copy(
                buffer.at[n, k], out.at[(index[0] + other) % 2, :, rows], sem.at[n, k]
            )
            copy.start()
            copies.append(copy)
    for copy in copies:
        copy.wait()


def gather(index, *pieces):
    anywhere = pl.BlockSpec(memory_space=pl.ANY)
    return pl.pallas_call(
        gather_kernel,
        in_specs=[smem()] + [anywhere] * 8,
        out_specs=anywhere,
        out_shape=shape_of(2, MODES, FRAME, FRAME),
        scratch_shapes=[
            pltpu.VMEM((8, 2, 8, MODES, 8, HALF), F32),
            pltpu.VMEM((8, 2, MODES, 32, FRAME), F32),
            pltpu.SemaphoreType.DMA((8,)),
            pltpu.SemaphoreType.DMA((8, 2)),
        ],
        compiler_params=PARAMS,
    )(index, *pieces)


def shifted(value, axis, steps):
    count = lax.axis_size(axis)
    first, last = (max(0, -steps), min(count, count - steps))
    return lax.ppermute(value, axis, [(source, source + steps) for source in range(first, last)])


def flip_patterns(patterns):
    rows = jnp.concatenate([patterns[:, :HALF], jnp.flip(patterns[:, HALF:], 1)], axis=1)
    return jnp.concatenate([rows[:, :, :HALF], jnp.flip(rows[:, :, HALF:], 2)], axis=2)


def swap_y(value, bits):
    return lax.ppermute(value, "row", [(r, r ^ (2 * bits)) for r in range(8)])


def swap_core(value):
    return lax.ppermute(value, "row", [(r, r ^ 1) for r in range(8)])


def per_device(object_field, probe_modes, patterns, offsets, counts):
    tabs, mod = tables()
    row_index, col = lax.axis_index("row"), lax.axis_index("col")
    y, core = row_index // 2, row_index % 2
    row = jnp.where(lax.iota(jnp.int32, 2) == 0, row_index, col)
    live = (lax.broadcasted_iota(jnp.int32, (3, 2), 1) < counts[0]).astype(jnp.int32)
    kind = lax.broadcasted_iota(jnp.int32, (3, 2), 0)
    slots = jnp.where(kind == 2, live, jnp.pad(offsets, ((0, 1), (0, 0))))

    right = shifted(object_field, "col", -1)
    below = shifted(object_field, "row", -1)
    diag = shifted(right, "row", -1)
    from_left = shifted(slots, "col", 1)
    from_up = shifted(slots, "row", 1)
    corner_pairs = [(r * 16 + c, r * 16 + c + 17) for r in range(7) for c in range(15)]
    from_corner = lax.ppermute(slots, ("row", "col"), corner_pairs)
    patt = flip_patterns(patterns)

    tiles = (object_field, right, below, diag)
    spec, ratio, q, power = forward(offsets, counts, tiles, mod, probe_modes, patt, tabs)
    common = (row, counts, spec, ratio, q, probe_modes)
    kept_a, sent_a, numer_a = inverse(*common, power, tabs, 0, 4)
    other_a = swap_core(sent_a)
    kept_b, sent_b, numer_b = inverse(*common, None, tabs, 4, 2)
    other_b = swap_core(sent_b)
    total_a = jnp.add(kept_a, other_a)
    y1_a = [swap_y(total_a[0, 2:], 1), swap_y(total_a[1, 2:], 3)]
    kept_c, sent_c, numer_c = inverse(*common, None, tabs, 6, 2)
    other_c = swap_core(sent_c)
    low, side, own = place(offsets, (numer_a, numer_b, numer_c), mod)
    total_c = jnp.concatenate([kept_b + other_b, kept_c + other_c], axis=3)
    y1_c = [swap_y(total_c[0, 2:], 1), swap_y(total_c[1, 2:], 3)]
    done_a = [jnp.add(total_a[i, :2], y1_a[i]) for i in range(2)]
    y2_a = [swap_y(done_a[0][1], 3), swap_y(done_a[1][1], 1)]
    done_c = [jnp.add(total_c[i, :2], y1_c[i]) for i in range(2)]
    y2_c = [swap_y(done_c[0][1], 3), swap_y(done_c[1][1], 1)]
    above = shifted(low, "row", 1)
    mine = jnp.concatenate(
        [
            jnp.concatenate([done_a[i][0] + y2_a[i], done_c[i][0] + y2_c[i]], axis=1)
            for i in range(2)
        ],
        axis=0,
    )
    exchange = lambda value: lax.all_to_all(value, "col", split_axis=0, concat_axis=0, tiled=True)
    parts = exchange(mine)
    sums = jnp.sum(parts, axis=0)
    gradient = jnp.concatenate([sums[:4], sums[5:]], axis=0)
    tile = y * 16 + col
    old = lax.dynamic_slice(
        probe_modes, (core, 0, tile // 2 * 8, tile % 2 * HALF), (1, MODES, 8, HALF)
    )[0]
    fresh = old + gradient / (sums[4] + PROBE_DELTA)
    spread = jnp.broadcast_to(fresh[None], (16,) + fresh.shape)
    from_side = shifted(side + above[1], "col", 1)
    piece = exchange(spread)
    a, b = piece[:8], piece[8:]
    pair_a = jnp.stack([a, swap_y(a, 3)])
    pair_b = jnp.stack([b, swap_y(b, 1)])
    last_a = swap_y(pair_a, 1)
    last_b = swap_y(pair_b, 3)
    far_a, far_b = swap_core(pair_a), swap_core(pair_b)
    end_a, end_b = swap_core(last_a), swap_core(last_b)
    pieces = (pair_a, pair_b, far_a, far_b, last_a, last_b, end_a, end_b)
    new_probe = gather(row, *pieces)

    light = light_of(slots, from_left, from_up, from_corner, probe_modes)
    updated, *edges = update(row, object_field, own, above, from_side, light)
    between = lambda count: [(i, i ^ 1) for i in range(count)]
    across = lambda count: [(i, ((i + 1) ^ 1) - 1) for i in range(1, count - 1)]
    arrived = [
        lax.ppermute(edges[0], "row", between(8)),
        lax.ppermute(edges[1], "row", across(8)),
        lax.ppermute(edges[2], "col", between(16)),
        lax.ppermute(edges[3], "col", across(16)),
    ]
    new_object = smooth(row, updated, *arrived)
    return (new_object, new_probe)


def solution(mesh):
    return jax.shard_map(
        per_device,
        mesh=mesh,
        in_specs=(
            P(None, "row", "col"),
            P(),
            P(("row", "col"), None, None),
            P(None, ("row", "col")),
            P(("row", "col")),
        ),
        out_specs=(P(None, "row", "col"), P()),
        check_vma=False,
    )
```

```python
import math

import jax
import jax.numpy as jnp
import numpy as np
from jax import lax
from jax.experimental import pallas as pl
from jax.experimental.pallas import tpu as pltpu
from jax.sharding import PartitionSpec as P

INTENSITY_FLOOR = 0.1
OBJECT_DELTA = 0.5
PROBE_DELTA = 1.0
SMOOTH_WEIGHT = 0.1
FRAME = 256
HALF = 128
MODES = 8
F32 = jnp.float32
BF16 = jnp.bfloat16
PARAMS = pltpu.CompilerParams(vmem_limit_bytes=58 * 1024 * 1024)


def tables():
    k = np.arange(HALF)[:, None] + 0.5
    x = np.arange(FRAME)[None, :]
    angle = 2.0 * math.pi * k * x / FRAME
    packed = np.concatenate([np.cos(angle), np.sin(angle)], axis=0) / math.sqrt(FRAME)
    high = packed.astype(np.float32).astype(jnp.bfloat16)
    low = (packed - high.astype(np.float64)).astype(np.float32).astype(jnp.bfloat16)
    ramp = np.arange(FRAME)
    phase = math.pi * (ramp[:, None] + ramp[None, :]) / FRAME
    mod = np.stack([np.cos(phase), np.sin(phase)]).astype(np.float32)
    return (high, low, high.T.copy(), low.T.copy()), mod


def full(*shape):
    return pl.BlockSpec(shape, lambda m: (0,) * len(shape))


def smem():
    return pl.BlockSpec(memory_space=pltpu.SMEM)


def vmem():
    return pl.BlockSpec(memory_space=pltpu.VMEM)


def shape_of(*shape):
    return jax.ShapeDtypeStruct(shape, F32)


def split(value):
    high = value.astype(BF16)
    return high, (value - high.astype(F32)).astype(BF16)


def mm(a, b):
    return jnp.dot(a, b, preferred_element_type=F32)


def two_sided(real, imag, left, right):
    parts = []
    for value in (real, imag):
        high, low = split(value)
        parts.append(mm(high, right[0]) + mm(low, right[0]) + mm(high, right[1]))
    results = []
    for part in parts:
        high, low = split(part)
        both = mm(left[0], high)
        results.append(both[:FRAME] + both[FRAME:] + mm(left[1], low))
    return results


def quarters(value):
    return value[:HALF, :HALF], value[:HALF, HALF:], value[HALF:, :HALF], value[HALF:, HALF:]


def grids():
    rows = lax.broadcasted_iota(jnp.int32, (FRAME, FRAME), 0)
    cols = lax.broadcasted_iota(jnp.int32, (FRAME, FRAME), 1)
    return rows, cols


def rolled(value, r, c):
    return pltpu.roll(pltpu.roll(value, r, axis=0), c, axis=1)


def spot(offsets, s):
    return offsets[0, s] & (FRAME - 1), offsets[1, s] & (FRAME - 1)


def alive(counts, s):
    return (s < counts[0]).astype(F32)


def forward_kernel(
    offsets, counts, own, right, below, diag_a, diag_b, mod, probe, patt, ph, plo, pth, ptl, spec, ratio, q, power, inten
):
    m = pl.program_id(0)

    @pl.when(m == 0)
    def _():
        rows, cols = grids()
        total = jnp.zeros((FRAME, FRAME), F32)
        for s in range(2):
            r, c = spot(offsets, s)
            parts = []
            for i in range(2):
                diag = jnp.concatenate([diag_a[i], diag_b[i]], axis=0)
                top = jnp.where(cols < c, right[i], own[i])
                bottom = jnp.where(cols < c, diag, below[i])
                tile = jnp.where(rows < r, bottom, top)
                parts.append(rolled(tile, lax.rem(FRAME - r, FRAME), lax.rem(FRAME - c, FRAME)))
            a, b = parts
            total = total + alive(counts, s) * (a * a + b * b)
            q[s, 0] = a * mod[0] - b * mod[1]
            q[s, 1] = a * mod[1] + b * mod[0]
            inten[s] = jnp.zeros((FRAME, FRAME), F32)
        power[...] = total

    pr, pi = probe[0, 0], probe[1, 0]
    for s in range(2):
        qr, qi = q[s, 0], q[s, 1]
        wr, wi = pr * qr - pi * qi, pr * qi + pi * qr
        mr, mi = two_sided(wr, wi, (jnp.concatenate([ph[...], plo[...]], axis=0), ph[...]), (pth[...], ptl[...]))
        acc, acs, asc, ass = quarters(mr)
        bcc, bcs, bsc, bss = quarters(mi)
        e1, e2 = acc - ass, acc + ass
        f1, f2 = bcs + bsc, bsc - bcs
        g1, g2 = bcc - bss, bcc + bss
        h1, h2 = acs + asc, acs - asc
        quads = (
            (0, 0, e1 + f1, g1 - h1),
            (0, HALF, e2 + f2, g2 + h2),
            (HALF, 0, e2 - f2, g2 - h2),
            (HALF, HALF, e1 - f1, g1 + h1),
        )
        for y, x, re, im in quads:
            spec[s, 0, 0, pl.ds(y, HALF), pl.ds(x, HALF)] = re
            spec[s, 0, 1, pl.ds(y, HALF), pl.ds(x, HALF)] = im
            inten[s, pl.ds(y, HALF), pl.ds(x, HALF)] += re * re + im * im

    @pl.when(m == MODES - 1)
    def _():
        for s in range(2):
            ratio[s] = patt[s] / jnp.sqrt(jnp.maximum(inten[s], INTENSITY_FLOOR))


def forward(offsets, counts, tiles, mod, probe, patt, tabs):
    return pl.pallas_call(
        forward_kernel,
        grid=(MODES,),
        in_specs=[smem()] * 2
        + [full(2, FRAME, FRAME)] * 3
        + [full(2, HALF, FRAME)] * 2
        + [full(2, FRAME, FRAME)]
        + [pl.BlockSpec((2, 1, FRAME, FRAME), lambda m: (0, m, 0, 0)), full(2, FRAME, FRAME)]
        + [full(FRAME, FRAME)] * 4,
        out_specs=[
            pl.BlockSpec((2, 1, 2, FRAME, FRAME), lambda m: (0, m, 0, 0, 0)),
            full(2, FRAME, FRAME),
            full(2, 2, FRAME, FRAME),
            full(FRAME, FRAME),
        ],
        out_shape=[
            shape_of(2, MODES, 2, FRAME, FRAME),
            shape_of(2, FRAME, FRAME),
            shape_of(2, 2, FRAME, FRAME),
            shape_of(FRAME, FRAME),
        ],
        scratch_shapes=[pltpu.VMEM((2, FRAME, FRAME), F32)],
        compiler_params=PARAMS,
    )(offsets, counts, *tiles, mod, probe, patt, *tabs)


def quarter_place(row, part, t):
    v = (t // 16) ^ (row[0] // 2)
    if part == 1:
        return v ^ (v >> 1)
    return jnp.where(v == 0, 0, jnp.where(v == 3, 1, v + 1))


def put_tiles(row, ref, value):
    for t in range(64):
        part, place = t % 16 // 8, t % 8
        where = quarter_place(row, part, t)
        i, j = t // 2, t % 2
        ref[part, where, place, 0] = value[8 * i : 8 * i + 8, HALF * j : HALF * j + HALF]


def inverse_kernel(count, row, counts, spec, ratio, q, probe, power, ph, plo, pth, ptl, kept, sent, numer):
    m = pl.program_id(0)

    @pl.when(m == 0)
    def _():
        numer[...] = jnp.zeros_like(numer)

    def one_mode():
        pr, pi = probe[0, 0], probe[1, 0]
        gr = jnp.zeros((FRAME, FRAME), F32)
        gi = jnp.zeros((FRAME, FRAME), F32)
        for s in range(2):
            live = alive(counts, s)
            rq = quarters(ratio[s])
            re = [a * b for a, b in zip(quarters(spec[s, 0, 0]), rq)]
            im = [a * b for a, b in zip(quarters(spec[s, 0, 1]), rq)]
            s1r, d1r, s2r, d2r = re[0] + re[3], re[0] - re[3], re[1] + re[2], re[1] - re[2]
            s1i, d1i, s2i, d2i = im[0] + im[3], im[3] - im[0], im[1] + im[2], im[1] - im[2]
            join = lambda a, b, axis: jnp.concatenate([a, b], axis=axis)
            ur = join(join(s1r + s2r, d1i + d2i, 1), join(d1i - d2i, s2r - s1r, 1), 0)
            ui = join(join(s1i + s2i, d1r - d2r, 1), join(d1r + d2r, s2i - s1i, 1), 0)
            nr, ni = two_sided(ur, ui, (jnp.concatenate([pth[...], ptl[...]], axis=0), pth[...]), (ph[...], plo[...]))
            qr, qi = q[s, 0], q[s, 1]
            dr = (nr - (pr * qr - pi * qi)) * live
            di = (ni - (pr * qi + pi * qr)) * live
            numer[s, 0] += pr * dr + pi * di
            numer[s, 1] += pr * di - pi * dr
            gr = gr + (qr * dr + qi * di)
            gi = gi + (qr * di - qi * dr)
        first_core = row[0] % 2 == 0
        put_tiles(row, kept, jnp.where(first_core, gr, gi))
        put_tiles(row, sent, jnp.where(first_core, gi, gr))

    if power is None:
        one_mode()
    else:
        pl.when(m < count)(one_mode)

        @pl.when(m == count)
        def _():
            put_tiles(row, kept, power[...])
            put_tiles(row, sent, power[...])


def inverse(row, counts, spec, ratio, q, probe, power, tabs, first, count):
    planes = count if power is None else count + 1
    last = first + count - 1
    mode = lambda m: jnp.minimum(m + first, last)
    if power is None:
        body = lambda *refs: inverse_kernel(count, *refs[:6], None, *refs[6:])
    else:
        body = lambda *refs: inverse_kernel(count, *refs)
    return pl.pallas_call(
        body,
        grid=(planes,),
        in_specs=[
            smem(),
            smem(),
            pl.BlockSpec((2, 1, 2, FRAME, FRAME), lambda m: (0, mode(m), 0, 0, 0)),
            full(2, FRAME, FRAME),
            full(2, 2, FRAME, FRAME),
            pl.BlockSpec((2, 1, FRAME, FRAME), lambda m: (0, mode(m), 0, 0)),
        ]
        + ([] if power is None else [full(FRAME, FRAME)])
        + [full(FRAME, FRAME)] * 4,
        out_specs=[
            pl.BlockSpec((2, 4, 8, 1, 8, HALF), lambda m: (0, 0, 0, m, 0, 0)),
            pl.BlockSpec((2, 4, 8, 1, 8, HALF), lambda m: (0, 0, 0, m, 0, 0)),
            full(2, 2, FRAME, FRAME),
        ],
        out_shape=[shape_of(2, 4, 8, planes, 8, HALF)] * 2 + [shape_of(2, 2, FRAME, FRAME)],
        compiler_params=PARAMS,
    )(row, counts, spec, ratio, q, probe, *([] if power is None else [power]), *tabs)


def light_kernel(offsets, left, up, corner, probe, light):
    power = jnp.zeros((FRAME, FRAME), F32)
    for m in range(MODES):
        power = power + (probe[0, m] * probe[0, m] + probe[1, m] * probe[1, m])
    rows, cols = grids()
    total = jnp.zeros((FRAME, FRAME), F32)
    for source, low_row, low_col in ((offsets, 0, 0), (left, 0, 1), (up, 1, 0), (corner, 1, 1)):
        for s in range(2):
            r, c = spot(source, s)
            keep = ((rows < r) if low_row else (rows >= r)) & ((cols < c) if low_col else (cols >= c))
            moved = source[2, s].astype(F32) * rolled(power, r, c)
            total = total + jnp.where(keep, moved, 0.0)
    light[...] = total


def light_of(offsets, left, up, corner, probe):
    return pl.pallas_call(
        light_kernel,
        in_specs=[smem()] * 4 + [vmem()],
        out_specs=vmem(),
        out_shape=shape_of(FRAME, FRAME),
        compiler_params=PARAMS,
    )(offsets, left, up, corner, probe)


def place_kernel(offsets, n0, n1, n2, mod, low, side, own):
    rows, cols = grids()
    pieces = []
    for s in range(2):
        r, c = spot(offsets, s)
        a, b = (n0[s, i] + n1[s, i] + n2[s, i] for i in range(2))
        real = rolled(a * mod[0] + b * mod[1], r, c)
        imag = rolled(b * mod[0] - a * mod[1], r, c)
        pieces.append((rows < r, cols < c, (real, imag)))
    for tile, out in ((2, low.at[0]), (3, low.at[1]), (1, side), (0, own)):
        for i in range(2):
            total = jnp.zeros((FRAME, FRAME), F32)
            for low_row, low_col, values in pieces:
                keep = (low_row if tile // 2 else ~low_row) & (low_col if tile % 2 else ~low_col)
                total = total + jnp.where(keep, values[i], 0.0)
            out[i] = total


def place(offsets, numers, mod):
    return pl.pallas_call(
        place_kernel,
        in_specs=[smem()] + [vmem()] * 4,
        out_specs=[vmem()] * 3,
        out_shape=[shape_of(2, 2, FRAME, FRAME)] + [shape_of(2, FRAME, FRAME)] * 2,
        compiler_params=PARAMS,
    )(offsets, *numers, mod)


def update_kernel(index, field, own, above, left, light, out, row_1, row_2, col_1, col_2):
    odd_row, odd_col = index[0] % 2 == 1, index[1] % 2 == 1
    inverse_light = 1.0 / (light[...] + OBJECT_DELTA)
    for i in range(2):
        value = field[i] + (own[i] + above[0, i] + left[i]) * inverse_light
        out[i] = value
        top, bottom = value[0], value[FRAME - 1]
        first, last = value[:, :HALF].T[0], value[:, HALF:].T[HALF - 1]
        row_1[i] = jnp.where(odd_row, top, bottom)
        row_2[i] = jnp.where(odd_row, bottom, top)
        col_1[i] = jnp.where(odd_col, first, last)
        col_2[i] = jnp.where(odd_col, last, first)


def update(index, field, own, above, left, light):
    return pl.pallas_call(
        update_kernel,
        in_specs=[smem()] + [vmem()] * 5,
        out_specs=[vmem()] * 5,
        out_shape=[shape_of(2, FRAME, FRAME)] + [shape_of(2, FRAME)] * 4,
        compiler_params=PARAMS,
    )(index, field, own, above, left, light)


def smooth_kernel(index, field, row_1, row_2, col_1, col_2, out):
    odd_row, odd_col = index[0] % 2 == 1, index[1] % 2 == 1
    rows, cols = grids()
    for i in range(2):
        value = field[i]
        above = jnp.where(odd_row, row_1[i], row_2[i])[None, :]
        below = jnp.where(odd_row, row_2[i], row_1[i])[None, :]
        column = lambda edge: jnp.broadcast_to(edge[None, :], (HALF, FRAME)).T
        wide = lambda edge: jnp.concatenate([column(edge), column(edge)], axis=1)
        left = wide(jnp.where(odd_col, col_1[i], col_2[i]))
        right = wide(jnp.where(odd_col, col_2[i], col_1[i]))
        north = jnp.where(rows == 0, above, pltpu.roll(value, 1, axis=0))
        south = jnp.where(rows == FRAME - 1, below, pltpu.roll(value, FRAME - 1, axis=0))
        west = jnp.where(cols == 0, left, pltpu.roll(value, 1, axis=1))
        east = jnp.where(cols == FRAME - 1, right, pltpu.roll(value, FRAME - 1, axis=1))
        out[i] = value + SMOOTH_WEIGHT * (north + south + east + west - 4.0 * value)


def smooth(index, field, *edges):
    return pl.pallas_call(
        smooth_kernel,
        in_specs=[smem()] + [vmem()] * 5,
        out_specs=vmem(),
        out_shape=shape_of(2, FRAME, FRAME),
        compiler_params=PARAMS,
    )(index, field, *edges)


ORDER = ((0, 3, 1, 2), (0, 1, 3, 2))


def gather_kernel(half, index, *refs):
    out, buffer, sem, loaded, load_sem = refs[-5:]
    copies = []
    loads = [pltpu.make_async_copy(refs[n], loaded.at[n], load_sem.at[n]) for n in range(4)]
    for load in loads:
        load.start()
    for other in range(2):
        target = (index[0] + other) % 2
        for part in range(2):
            loads[2 * other + part].wait()
            piece = loaded.at[2 * other + part]
            for k in range(2):
                for m in range(MODES):
                    for place in range(8):
                        i, j = place // 2, place % 2
                        buffer[
                            other, part, k, m, 8 * i : 8 * i + 8, HALF * j : HALF * j + HALF
                        ] = piece[k, place, m]
                quarter = ORDER[part][2 * half + k] ^ (index[0] // 2)
                rows = pl.ds(pl.multiple_of(64 * quarter + 32 * part, 32), 32)
                copy = pltpu.make_async_copy(
                    buffer.at[other, part, k], out.at[target, :, rows], sem.at[other, part, k]
                )
                copy.start()
                copies.append(copy)
    for copy in copies:
        copy.wait()


def gather(index, pieces, half, target=None):
    anywhere = pl.BlockSpec(memory_space=pl.ANY)
    return pl.pallas_call(
        lambda *refs: gather_kernel(half, *refs),
        in_specs=[smem()] + [anywhere] * (4 if target is None else 5),
        out_specs=anywhere,
        out_shape=shape_of(2, MODES, FRAME, FRAME),
        scratch_shapes=[
            pltpu.VMEM((2, 2, 2, MODES, 32, FRAME), F32),
            pltpu.SemaphoreType.DMA((2, 2, 2)),
            pltpu.VMEM((4, 2, 8, MODES, 8, HALF), F32),
            pltpu.SemaphoreType.DMA((4,)),
        ],
        input_output_aliases={} if target is None else {5: 0},
        compiler_params=PARAMS,
    )(index, *pieces, *([] if target is None else [target]))


def shifted(value, axis, steps):
    count = lax.axis_size(axis)
    first, last = (max(0, -steps), min(count, count - steps))
    return lax.ppermute(value, axis, [(source, source + steps) for source in range(first, last)])


def flip_patterns(patterns):
    rows = jnp.concatenate([patterns[:, :HALF], jnp.flip(patterns[:, HALF:], 1)], axis=1)
    return jnp.concatenate([rows[:, :, :HALF], jnp.flip(rows[:, :, HALF:], 2)], axis=2)


def swap_y(value, bits):
    return lax.ppermute(value, "row", [(r, r ^ (2 * bits)) for r in range(8)])


def swap_core(value):
    return lax.ppermute(value, "row", [(r, r ^ 1) for r in range(8)])


def per_device(object_field, probe_modes, patterns, offsets, counts):
    tabs, mod = tables()
    row_index, col = lax.axis_index("row"), lax.axis_index("col")
    y, core = row_index // 2, row_index % 2
    row = jnp.where(lax.iota(jnp.int32, 2) == 0, row_index, col)
    live = (lax.broadcasted_iota(jnp.int32, (3, 2), 1) < counts[0]).astype(jnp.int32)
    kind = lax.broadcasted_iota(jnp.int32, (3, 2), 0)
    slots = jnp.where(kind == 2, live, jnp.pad(offsets, ((0, 1), (0, 0))))

    right = shifted(object_field, "col", -1)
    below = shifted(object_field, "row", -1)
    diag_a = shifted(right[:, :HALF], "row", -1)
    diag_b = shifted(below[:, HALF:], "col", -1)
    from_left = shifted(slots, "col", 1)
    from_up = shifted(slots, "row", 1)
    corner_pairs = [(r * 16 + c, r * 16 + c + 17) for r in range(7) for c in range(15)]
    from_corner = lax.ppermute(slots, ("row", "col"), corner_pairs)
    patt = flip_patterns(patterns)

    tiles = (object_field, right, below, diag_a, diag_b)
    spec, ratio, q, power = forward(offsets, counts, tiles, mod, probe_modes, patt, tabs)
    common = (row, counts, spec, ratio, q, probe_modes)
    kept_a, sent_a, numer_a = inverse(*common, power, tabs, 0, 4)
    other_a = swap_core(sent_a)
    kept_b, sent_b, numer_b = inverse(*common, None, tabs, 4, 2)
    other_b = swap_core(sent_b)
    total_a = jnp.add(kept_a, other_a)
    y1_a = [swap_y(total_a[0, 2:], 1), swap_y(total_a[1, 2:], 3)]
    kept_c, sent_c, numer_c = inverse(*common, None, tabs, 6, 2)
    other_c = swap_core(sent_c)
    low, side, own = place(offsets, (numer_a, numer_b, numer_c), mod)
    total_c = jnp.concatenate([kept_b + other_b, kept_c + other_c], axis=3)
    y1_c = [swap_y(total_c[0, 2:], 1), swap_y(total_c[1, 2:], 3)]
    done_a = [jnp.add(total_a[i, :2], y1_a[i]) for i in range(2)]
    y2_a = [swap_y(done_a[0][1], 3), swap_y(done_a[1][1], 1)]
    done_c = [jnp.add(total_c[i, :2], y1_c[i]) for i in range(2)]
    y2_c = [swap_y(done_c[0][1], 3), swap_y(done_c[1][1], 1)]
    above = shifted(low, "row", 1)
    mine = jnp.concatenate(
        [
            jnp.concatenate([done_a[i][0] + y2_a[i], done_c[i][0] + y2_c[i]], axis=1)
            for i in range(2)
        ],
        axis=0,
    )
    exchange = lambda value: lax.all_to_all(value, "col", split_axis=0, concat_axis=0, tiled=True)
    parts = exchange(mine)
    sums = jnp.sum(parts, axis=0)
    gradient = jnp.concatenate([sums[:4], sums[5:]], axis=0)
    tile = y * 16 + col
    old = lax.dynamic_slice(
        probe_modes, (core, 0, tile // 2 * 8, tile % 2 * HALF), (1, MODES, 8, HALF)
    )[0]
    fresh = old + gradient / (sums[4] + PROBE_DELTA)
    spread = jnp.broadcast_to(fresh[None], (16,) + fresh.shape)
    from_side = shifted(side + above[1], "col", 1)
    piece = exchange(spread)
    a, b = piece[:8], piece[8:]
    pair_a = jnp.stack([a, swap_y(a, 3)])
    pair_b = jnp.stack([b, swap_y(b, 1)])
    last_a = swap_y(pair_a, 1)
    last_b = swap_y(pair_b, 3)
    far_a, far_b = swap_core(pair_a), swap_core(pair_b)
    end_a, end_b = swap_core(last_a), swap_core(last_b)
    half_probe = gather(row, (pair_a, pair_b, far_a, far_b), 0)
    new_probe = gather(row, (last_a, last_b, end_a, end_b), 1, half_probe)

    light = light_of(slots, from_left, from_up, from_corner, probe_modes)
    updated, *edges = update(row, object_field, own, above, from_side, light)
    between = lambda count: [(i, i ^ 1) for i in range(count)]
    across = lambda count: [(i, ((i + 1) ^ 1) - 1) for i in range(1, count - 1)]
    arrived = [
        lax.ppermute(edges[0], "row", between(8)),
        lax.ppermute(edges[1], "row", across(8)),
        lax.ppermute(edges[2], "col", between(16)),
        lax.ppermute(edges[3], "col", across(16)),
    ]
    new_object = smooth(row, updated, *arrived)
    return (new_object, new_probe)


def solution(mesh):
    return jax.shard_map(
        per_device,
        mesh=mesh,
        in_specs=(
            P(None, "row", "col"),
            P(),
            P(("row", "col"), None, None),
            P(None, ("row", "col")),
            P(("row", "col")),
        ),
        out_specs=(P(None, "row", "col"), P()),
        check_vma=False,
    )
```

```python
import math

import jax
import jax.numpy as jnp
import numpy as np
from jax import lax
from jax.experimental import pallas as pl
from jax.experimental.pallas import tpu as pltpu
from jax.sharding import PartitionSpec as P

INTENSITY_FLOOR = 0.1
OBJECT_DELTA = 0.5
PROBE_DELTA = 1.0
SMOOTH_WEIGHT = 0.1
FRAME = 256
HALF = 128
MODES = 8
F32 = jnp.float32
BF16 = jnp.bfloat16
PARAMS = pltpu.CompilerParams(vmem_limit_bytes=58 * 1024 * 1024)


def tables():
    k = np.arange(HALF)[:, None] + 0.5
    x = np.arange(FRAME)[None, :]
    angle = 2.0 * math.pi * k * x / FRAME
    packed = np.concatenate([np.cos(angle), np.sin(angle)], axis=0) / math.sqrt(FRAME)
    high = packed.astype(np.float32).astype(jnp.bfloat16)
    low = (packed - high.astype(np.float64)).astype(np.float32).astype(jnp.bfloat16)
    ramp = np.arange(FRAME)
    phase = math.pi * (ramp[:, None] + ramp[None, :]) / FRAME
    mod = np.stack([np.cos(phase), np.sin(phase)]).astype(np.float32)
    return (high, low, high.T.copy(), low.T.copy()), mod


def full(*shape):
    return pl.BlockSpec(shape, lambda m: (0,) * len(shape))


def smem():
    return pl.BlockSpec(memory_space=pltpu.SMEM)


def vmem():
    return pl.BlockSpec(memory_space=pltpu.VMEM)


def shape_of(*shape):
    return jax.ShapeDtypeStruct(shape, F32)


def split(value):
    high = value.astype(BF16)
    return high, (value - high.astype(F32)).astype(BF16)


def mm(a, b):
    return jnp.dot(a, b, preferred_element_type=F32)


def two_sided(real, imag, left, right):
    parts = []
    for value in (real, imag):
        high, low = split(value)
        parts.append(mm(high, right[0]) + mm(low, right[0]) + mm(high, right[1]))
    results = []
    for part in parts:
        high, low = split(part)
        both = mm(left[0], high)
        results.append(both[:FRAME] + both[FRAME:] + mm(left[1], low))
    return results


def quarters(value):
    return value[:HALF, :HALF], value[:HALF, HALF:], value[HALF:, :HALF], value[HALF:, HALF:]


def grids():
    rows = lax.broadcasted_iota(jnp.int32, (FRAME, FRAME), 0)
    cols = lax.broadcasted_iota(jnp.int32, (FRAME, FRAME), 1)
    return rows, cols


def rolled(value, r, c):
    return pltpu.roll(pltpu.roll(value, r, axis=0), c, axis=1)


def spot(offsets, s):
    return offsets[0, s] & (FRAME - 1), offsets[1, s] & (FRAME - 1)


def alive(counts, s):
    return (s < counts[0]).astype(F32)


def forward_kernel(
    offsets, counts, own, right, below, diag_a, diag_b, mod, probe, patt, ph, plo, pth, ptl, spec, ratio, q, power, inten
):
    m = pl.program_id(0)

    @pl.when(m == 0)
    def _():
        rows, cols = grids()
        total = jnp.zeros((FRAME, FRAME), F32)
        for s in range(2):
            r, c = spot(offsets, s)
            parts = []
            for i in range(2):
                diag = jnp.concatenate([diag_a[i], diag_b[i]], axis=0)
                top = jnp.where(cols < c, right[i], own[i])
                bottom = jnp.where(cols < c, diag, below[i])
                tile = jnp.where(rows < r, bottom, top)
                parts.append(rolled(tile, lax.rem(FRAME - r, FRAME), lax.rem(FRAME - c, FRAME)))
            a, b = parts
            total = total + alive(counts, s) * (a * a + b * b)
            q[s, 0] = a * mod[0] - b * mod[1]
            q[s, 1] = a * mod[1] + b * mod[0]
            inten[s] = jnp.zeros((FRAME, FRAME), F32)
        power[...] = total

    pr, pi = probe[0, 0], probe[1, 0]
    for s in range(2):
        qr, qi = q[s, 0], q[s, 1]
        wr, wi = pr * qr - pi * qi, pr * qi + pi * qr
        mr, mi = two_sided(wr, wi, (jnp.concatenate([ph[...], plo[...]], axis=0), ph[...]), (pth[...], ptl[...]))
        acc, acs, asc, ass = quarters(mr)
        bcc, bcs, bsc, bss = quarters(mi)
        e1, e2 = acc - ass, acc + ass
        f1, f2 = bcs + bsc, bsc - bcs
        g1, g2 = bcc - bss, bcc + bss
        h1, h2 = acs + asc, acs - asc
        quads = (
            (0, 0, e1 + f1, g1 - h1),
            (0, HALF, e2 + f2, g2 + h2),
            (HALF, 0, e2 - f2, g2 - h2),
            (HALF, HALF, e1 - f1, g1 + h1),
        )
        for y, x, re, im in quads:
            spec[s, 0, 0, pl.ds(y, HALF), pl.ds(x, HALF)] = re
            spec[s, 0, 1, pl.ds(y, HALF), pl.ds(x, HALF)] = im
            inten[s, pl.ds(y, HALF), pl.ds(x, HALF)] += re * re + im * im

    @pl.when(m == MODES - 1)
    def _():
        for s in range(2):
            ratio[s] = patt[s] / jnp.sqrt(jnp.maximum(inten[s], INTENSITY_FLOOR))


def forward(offsets, counts, tiles, mod, probe, patt, tabs):
    return pl.pallas_call(
        forward_kernel,
        grid=(MODES,),
        in_specs=[smem()] * 2
        + [full(2, FRAME, FRAME)] * 3
        + [full(2, HALF, FRAME)] * 2
        + [full(2, FRAME, FRAME)]
        + [pl.BlockSpec((2, 1, FRAME, FRAME), lambda m: (0, m, 0, 0)), full(2, FRAME, FRAME)]
        + [full(FRAME, FRAME)] * 4,
        out_specs=[
            pl.BlockSpec((2, 1, 2, FRAME, FRAME), lambda m: (0, m, 0, 0, 0)),
            full(2, FRAME, FRAME),
            full(2, 2, FRAME, FRAME),
            full(FRAME, FRAME),
        ],
        out_shape=[
            shape_of(2, MODES, 2, FRAME, FRAME),
            shape_of(2, FRAME, FRAME),
            shape_of(2, 2, FRAME, FRAME),
            shape_of(FRAME, FRAME),
        ],
        scratch_shapes=[pltpu.VMEM((2, FRAME, FRAME), F32)],
        compiler_params=PARAMS,
    )(offsets, counts, *tiles, mod, probe, patt, *tabs)


def quarter_place(row, part, t):
    v = (t // 16) ^ (row[0] // 2)
    if part == 1:
        return v ^ (v >> 1)
    return jnp.where(v == 0, 0, jnp.where(v == 3, 1, v + 1))


def put_tiles(row, ref, value):
    for t in range(64):
        part, place = t % 16 // 8, t % 8
        where = quarter_place(row, part, t)
        i, j = t // 2, t % 2
        ref[part, where, place, 0] = value[8 * i : 8 * i + 8, HALF * j : HALF * j + HALF]


def inverse_kernel(count, row, counts, spec, ratio, q, probe, power, ph, plo, pth, ptl, kept, sent, numer):
    m = pl.program_id(0)

    @pl.when(m == 0)
    def _():
        numer[...] = jnp.zeros_like(numer)

    def one_mode():
        pr, pi = probe[0, 0], probe[1, 0]
        gr = jnp.zeros((FRAME, FRAME), F32)
        gi = jnp.zeros((FRAME, FRAME), F32)
        for s in range(2):
            live = alive(counts, s)
            rq = quarters(ratio[s])
            re = [a * b for a, b in zip(quarters(spec[s, 0, 0]), rq)]
            im = [a * b for a, b in zip(quarters(spec[s, 0, 1]), rq)]
            s1r, d1r, s2r, d2r = re[0] + re[3], re[0] - re[3], re[1] + re[2], re[1] - re[2]
            s1i, d1i, s2i, d2i = im[0] + im[3], im[3] - im[0], im[1] + im[2], im[1] - im[2]
            join = lambda a, b, axis: jnp.concatenate([a, b], axis=axis)
            ur = join(join(s1r + s2r, d1i + d2i, 1), join(d1i - d2i, s2r - s1r, 1), 0)
            ui = join(join(s1i + s2i, d1r - d2r, 1), join(d1r + d2r, s2i - s1i, 1), 0)
            nr, ni = two_sided(ur, ui, (jnp.concatenate([pth[...], ptl[...]], axis=0), pth[...]), (ph[...], plo[...]))
            qr, qi = q[s, 0], q[s, 1]
            dr = (nr - (pr * qr - pi * qi)) * live
            di = (ni - (pr * qi + pi * qr)) * live
            numer[s, 0] += pr * dr + pi * di
            numer[s, 1] += pr * di - pi * dr
            gr = gr + (qr * dr + qi * di)
            gi = gi + (qr * di - qi * dr)
        first_core = row[0] % 2 == 0
        put_tiles(row, kept, jnp.where(first_core, gr, gi))
        put_tiles(row, sent, jnp.where(first_core, gi, gr))

    if power is None:
        one_mode()
    else:
        pl.when(m < count)(one_mode)

        @pl.when(m == count)
        def _():
            put_tiles(row, kept, power[...])
            put_tiles(row, sent, power[...])


def inverse(row, counts, spec, ratio, q, probe, power, tabs, first, count):
    planes = count if power is None else count + 1
    last = first + count - 1
    mode = lambda m: jnp.minimum(m + first, last)
    if power is None:
        body = lambda *refs: inverse_kernel(count, *refs[:6], None, *refs[6:])
    else:
        body = lambda *refs: inverse_kernel(count, *refs)
    return pl.pallas_call(
        body,
        grid=(planes,),
        in_specs=[
            smem(),
            smem(),
            pl.BlockSpec((2, 1, 2, FRAME, FRAME), lambda m: (0, mode(m), 0, 0, 0)),
            full(2, FRAME, FRAME),
            full(2, 2, FRAME, FRAME),
            pl.BlockSpec((2, 1, FRAME, FRAME), lambda m: (0, mode(m), 0, 0)),
        ]
        + ([] if power is None else [full(FRAME, FRAME)])
        + [full(FRAME, FRAME)] * 4,
        out_specs=[
            pl.BlockSpec((2, 4, 8, 1, 8, HALF), lambda m: (0, 0, 0, m, 0, 0)),
            pl.BlockSpec((2, 4, 8, 1, 8, HALF), lambda m: (0, 0, 0, m, 0, 0)),
            full(2, 2, FRAME, FRAME),
        ],
        out_shape=[shape_of(2, 4, 8, planes, 8, HALF)] * 2 + [shape_of(2, 2, FRAME, FRAME)],
        compiler_params=PARAMS,
    )(row, counts, spec, ratio, q, probe, *([] if power is None else [power]), *tabs)


def light_kernel(offsets, left, up, corner, probe, light):
    power = jnp.zeros((FRAME, FRAME), F32)
    for m in range(MODES):
        power = power + (probe[0, m] * probe[0, m] + probe[1, m] * probe[1, m])
    rows, cols = grids()
    total = jnp.zeros((FRAME, FRAME), F32)
    for source, low_row, low_col in ((offsets, 0, 0), (left, 0, 1), (up, 1, 0), (corner, 1, 1)):
        for s in range(2):
            r, c = spot(source, s)
            keep = ((rows < r) if low_row else (rows >= r)) & ((cols < c) if low_col else (cols >= c))
            moved = source[2, s].astype(F32) * rolled(power, r, c)
            total = total + jnp.where(keep, moved, 0.0)
    light[...] = total


def light_of(offsets, left, up, corner, probe):
    return pl.pallas_call(
        light_kernel,
        in_specs=[smem()] * 4 + [vmem()],
        out_specs=vmem(),
        out_shape=shape_of(FRAME, FRAME),
        compiler_params=PARAMS,
    )(offsets, left, up, corner, probe)


def place_kernel(offsets, n0, n1, mod, low, side, own):
    rows, cols = grids()
    pieces = []
    for s in range(2):
        r, c = spot(offsets, s)
        a, b = (n0[s, i] + n1[s, i] for i in range(2))
        real = rolled(a * mod[0] + b * mod[1], r, c)
        imag = rolled(b * mod[0] - a * mod[1], r, c)
        pieces.append((rows < r, cols < c, (real, imag)))
    for tile, out in ((2, low.at[0]), (3, low.at[1]), (1, side), (0, own)):
        for i in range(2):
            total = jnp.zeros((FRAME, FRAME), F32)
            for low_row, low_col, values in pieces:
                keep = (low_row if tile // 2 else ~low_row) & (low_col if tile % 2 else ~low_col)
                total = total + jnp.where(keep, values[i], 0.0)
            out[i] = total


def place(offsets, numers, mod):
    return pl.pallas_call(
        place_kernel,
        in_specs=[smem()] + [vmem()] * 3,
        out_specs=[vmem()] * 3,
        out_shape=[shape_of(2, 2, FRAME, FRAME)] + [shape_of(2, FRAME, FRAME)] * 2,
        compiler_params=PARAMS,
    )(offsets, *numers, mod)


def update_kernel(index, field, own, above, left, light, out, row_1, row_2, col_1, col_2):
    odd_row, odd_col = index[0] % 2 == 1, index[1] % 2 == 1
    inverse_light = 1.0 / (light[...] + OBJECT_DELTA)
    for i in range(2):
        value = field[i] + (own[i] + above[0, i] + left[i]) * inverse_light
        out[i] = value
        top, bottom = value[0], value[FRAME - 1]
        first, last = value[:, :HALF].T[0], value[:, HALF:].T[HALF - 1]
        row_1[i] = jnp.where(odd_row, top, bottom)
        row_2[i] = jnp.where(odd_row, bottom, top)
        col_1[i] = jnp.where(odd_col, first, last)
        col_2[i] = jnp.where(odd_col, last, first)


def update(index, field, own, above, left, light):
    return pl.pallas_call(
        update_kernel,
        in_specs=[smem()] + [vmem()] * 5,
        out_specs=[vmem()] * 5,
        out_shape=[shape_of(2, FRAME, FRAME)] + [shape_of(2, FRAME)] * 4,
        compiler_params=PARAMS,
    )(index, field, own, above, left, light)


def smooth_kernel(index, field, row_1, row_2, col_1, col_2, out):
    odd_row, odd_col = index[0] % 2 == 1, index[1] % 2 == 1
    rows, cols = grids()
    for i in range(2):
        value = field[i]
        above = jnp.where(odd_row, row_1[i], row_2[i])[None, :]
        below = jnp.where(odd_row, row_2[i], row_1[i])[None, :]
        column = lambda edge: jnp.broadcast_to(edge[None, :], (HALF, FRAME)).T
        wide = lambda edge: jnp.concatenate([column(edge), column(edge)], axis=1)
        left = wide(jnp.where(odd_col, col_1[i], col_2[i]))
        right = wide(jnp.where(odd_col, col_2[i], col_1[i]))
        north = jnp.where(rows == 0, above, pltpu.roll(value, 1, axis=0))
        south = jnp.where(rows == FRAME - 1, below, pltpu.roll(value, FRAME - 1, axis=0))
        west = jnp.where(cols == 0, left, pltpu.roll(value, 1, axis=1))
        east = jnp.where(cols == FRAME - 1, right, pltpu.roll(value, FRAME - 1, axis=1))
        out[i] = value + SMOOTH_WEIGHT * (north + south + east + west - 4.0 * value)


def smooth(index, field, *edges):
    return pl.pallas_call(
        smooth_kernel,
        in_specs=[smem()] + [vmem()] * 5,
        out_specs=vmem(),
        out_shape=shape_of(2, FRAME, FRAME),
        compiler_params=PARAMS,
    )(index, field, *edges)


ORDER = ((0, 3, 1, 2), (0, 1, 3, 2))


def gather_kernel(half, index, *refs):
    out, buffer, sem, loaded, load_sem = refs[-5:]
    copies = []
    loads = [pltpu.make_async_copy(refs[n], loaded.at[n], load_sem.at[n]) for n in range(4)]
    for load in loads:
        load.start()
    for other in range(2):
        target = (index[0] + other) % 2
        for part in range(2):
            loads[2 * other + part].wait()
            piece = loaded.at[2 * other + part]
            for k in range(2):
                for m in range(MODES):
                    for place in range(8):
                        i, j = place // 2, place % 2
                        buffer[
                            other, part, k, m, 8 * i : 8 * i + 8, HALF * j : HALF * j + HALF
                        ] = piece[k, place, m]
                quarter = ORDER[part][2 * half + k] ^ (index[0] // 2)
                rows = pl.ds(pl.multiple_of(64 * quarter + 32 * part, 32), 32)
                copy = pltpu.make_async_copy(
                    buffer.at[other, part, k], out.at[target, :, rows], sem.at[other, part, k]
                )
                copy.start()
                copies.append(copy)
    for copy in copies:
        copy.wait()


def gather(index, pieces, half, target=None):
    anywhere = pl.BlockSpec(memory_space=pl.ANY)
    return pl.pallas_call(
        lambda *refs: gather_kernel(half, *refs),
        in_specs=[smem()] + [anywhere] * (4 if target is None else 5),
        out_specs=anywhere,
        out_shape=shape_of(2, MODES, FRAME, FRAME),
        scratch_shapes=[
            pltpu.VMEM((2, 2, 2, MODES, 32, FRAME), F32),
            pltpu.SemaphoreType.DMA((2, 2, 2)),
            pltpu.VMEM((4, 2, 8, MODES, 8, HALF), F32),
            pltpu.SemaphoreType.DMA((4,)),
        ],
        input_output_aliases={} if target is None else {5: 0},
        compiler_params=PARAMS,
    )(index, *pieces, *([] if target is None else [target]))


def shifted(value, axis, steps):
    count = lax.axis_size(axis)
    first, last = (max(0, -steps), min(count, count - steps))
    return lax.ppermute(value, axis, [(source, source + steps) for source in range(first, last)])


def flip_patterns(patterns):
    rows = jnp.concatenate([patterns[:, :HALF], jnp.flip(patterns[:, HALF:], 1)], axis=1)
    return jnp.concatenate([rows[:, :, :HALF], jnp.flip(rows[:, :, HALF:], 2)], axis=2)


def swap_y(value, bits):
    return lax.ppermute(value, "row", [(r, r ^ (2 * bits)) for r in range(8)])


def swap_core(value):
    return lax.ppermute(value, "row", [(r, r ^ 1) for r in range(8)])


def per_device(object_field, probe_modes, patterns, offsets, counts):
    tabs, mod = tables()
    row_index, col = lax.axis_index("row"), lax.axis_index("col")
    y, core = row_index // 2, row_index % 2
    row = jnp.where(lax.iota(jnp.int32, 2) == 0, row_index, col)
    live = (lax.broadcasted_iota(jnp.int32, (3, 2), 1) < counts[0]).astype(jnp.int32)
    kind = lax.broadcasted_iota(jnp.int32, (3, 2), 0)
    slots = jnp.where(kind == 2, live, jnp.pad(offsets, ((0, 1), (0, 0))))

    right = shifted(object_field, "col", -1)
    below = shifted(object_field, "row", -1)
    diag_a = shifted(right[:, :HALF], "row", -1)
    diag_b = shifted(below[:, HALF:], "col", -1)
    from_left = shifted(slots, "col", 1)
    from_up = shifted(slots, "row", 1)
    corner_pairs = [(r * 16 + c, r * 16 + c + 17) for r in range(7) for c in range(15)]
    from_corner = lax.ppermute(slots, ("row", "col"), corner_pairs)
    patt = flip_patterns(patterns)

    tiles = (object_field, right, below, diag_a, diag_b)
    spec, ratio, q, power = forward(offsets, counts, tiles, mod, probe_modes, patt, tabs)
    common = (row, counts, spec, ratio, q, probe_modes)
    kept_a, sent_a, numer_a = inverse(*common, power, tabs, 0, 4)
    other_a = swap_core(sent_a)
    total_a = jnp.add(kept_a, other_a)
    y1_a = [swap_y(total_a[0, 2:], 1), swap_y(total_a[1, 2:], 3)]
    kept_c, sent_c, numer_c = inverse(*common, None, tabs, 4, 4)
    other_c = swap_core(sent_c)
    low, side, own = place(offsets, (numer_a, numer_c), mod)
    total_c = jnp.add(kept_c, other_c)
    y1_c = [swap_y(total_c[0, 2:], 1), swap_y(total_c[1, 2:], 3)]
    done_a = [jnp.add(total_a[i, :2], y1_a[i]) for i in range(2)]
    y2_a = [swap_y(done_a[0][1], 3), swap_y(done_a[1][1], 1)]
    done_c = [jnp.add(total_c[i, :2], y1_c[i]) for i in range(2)]
    y2_c = [swap_y(done_c[0][1], 3), swap_y(done_c[1][1], 1)]
    above = shifted(low, "row", 1)
    mine = jnp.concatenate(
        [
            jnp.concatenate([done_a[i][0] + y2_a[i], done_c[i][0] + y2_c[i]], axis=1)
            for i in range(2)
        ],
        axis=0,
    )
    exchange = lambda value: lax.all_to_all(value, "col", split_axis=0, concat_axis=0, tiled=True)
    parts = exchange(mine)
    sums = jnp.sum(parts, axis=0)
    gradient = jnp.concatenate([sums[:4], sums[5:]], axis=0)
    tile = y * 16 + col
    old = lax.dynamic_slice(
        probe_modes, (core, 0, tile // 2 * 8, tile % 2 * HALF), (1, MODES, 8, HALF)
    )[0]
    fresh = old + gradient / (sums[4] + PROBE_DELTA)
    spread = jnp.broadcast_to(fresh[None], (16,) + fresh.shape)
    from_side = shifted(side + above[1], "col", 1)
    piece = exchange(spread)
    a, b = piece[:8], piece[8:]
    pair_a = jnp.stack([a, swap_y(a, 3)])
    pair_b = jnp.stack([b, swap_y(b, 1)])
    last_a = swap_y(pair_a, 1)
    last_b = swap_y(pair_b, 3)
    far_a, far_b = swap_core(pair_a), swap_core(pair_b)
    end_a, end_b = swap_core(last_a), swap_core(last_b)
    half_probe = gather(row, (pair_a, pair_b, far_a, far_b), 0)
    new_probe = gather(row, (last_a, last_b, end_a, end_b), 1, half_probe)

    light = light_of(slots, from_left, from_up, from_corner, probe_modes)
    updated, *edges = update(row, object_field, own, above, from_side, light)
    between = lambda count: [(i, i ^ 1) for i in range(count)]
    across = lambda count: [(i, ((i + 1) ^ 1) - 1) for i in range(1, count - 1)]
    arrived = [
        lax.ppermute(edges[0], "row", between(8)),
        lax.ppermute(edges[1], "row", across(8)),
        lax.ppermute(edges[2], "col", between(16)),
        lax.ppermute(edges[3], "col", across(16)),
    ]
    new_object = smooth(row, updated, *arrived)
    return (new_object, new_probe)


def solution(mesh):
    return jax.shard_map(
        per_device,
        mesh=mesh,
        in_specs=(
            P(None, "row", "col"),
            P(),
            P(("row", "col"), None, None),
            P(None, ("row", "col")),
            P(("row", "col")),
        ),
        out_specs=(P(None, "row", "col"), P()),
        check_vma=False,
    )
```
